32 devices in a mesh: row: 4 (over z), col: 2 (over x), rep: 4 (over y, core).
Axes of the slice: x: 2, y: 2, z: 4, core: 2. Of those that a mesh axis runs over, the one named last changes fastest.
Arguments:
- features: bfloat16 [8192, 256], P(('col', 'rep'), 'row'), may hold values from -6 to 6
- weight: bfloat16 [256, 256], replicated, may hold values from -0.375 to 0.375
- cotangent: bfloat16 [8192, 256], P(('row', 'col', 'rep')), may hold values from -6 to 6
- block_values: bfloat16 [4, 8, 128, 128, 128], P('row', ('col', 'rep')), may hold values from -0.0625 to 0.0625
- block_coords: int32 [4, 8, 128, 2], P('row', ('col', 'rep')), may hold values from 0 to 15, as said below
- block_counts: int32 [4, 8], P('row', ('col', 'rep')), may hold values from 1 to 128, as said below
Outputs:
- activations: bfloat16 [8192, 256], P(('row', 'col', 'rep'))
- input_grad: bfloat16 [8192, 256], P(('col', 'rep'), 'row')
- weight_grad: float32 [256, 256], replicated
The draws below stay inside these ranges and needn't reach their ends.
Inputs may be any that keep to these rules, and one draw needn't show every extreme that they name: `block_coords`: each slot's row block is below 16 and its column block below 8. `block_counts`: some tile uses all 128 slots.
All inputs are finite; a program needn't handle non-finite values.
Results may differ from the reference program's by a relative error of at most 0.014.
Values may be sent and summed in bfloat16 or wider, within the bound.
A program may use at most 128 MiB of HBM per device.

```python
import jax
import jax.numpy as jnp
from jax import lax

F = 256
NODE_DEV = 256
NODES = 8192
ROW_TILES = 4
COL_TILES = 8
TILE_RB = 16
TILE_CB = 8
NNZB = 128


def draw_block_coords(key, part):
    key_rows = jax.random.fold_in(key, 11)
    key_cols = jax.random.fold_in(key, 12)
    rows_at = jax.random.randint(key_rows, (ROW_TILES, COL_TILES, NNZB), 0, TILE_RB, dtype=jnp.int32)
    cols_at = jax.random.randint(key_cols, (ROW_TILES, COL_TILES, NNZB), 0, TILE_CB, dtype=jnp.int32)
    rows_at = rows_at.at[0, 0, 0].set(TILE_RB - 1)
    cols_at = cols_at.at[0, 0, 0].set(TILE_CB - 1)
    return jnp.stack([rows_at, cols_at], axis=-1)


def draw_block_counts(key, part):
    key_counts = jax.random.fold_in(key, 21)
    key_full = jax.random.fold_in(key, 22)
    lowest = max(1, NNZB // 8)
    counts = jax.random.randint(key_counts, (ROW_TILES * COL_TILES,), lowest, NNZB + 1, dtype=jnp.int32)
    full_at = jax.random.randint(key_full, (), 0, ROW_TILES * COL_TILES, dtype=jnp.int32)
    counts = counts.at[full_at].set(NNZB)
    return counts.reshape(ROW_TILES, COL_TILES)


def levels(rng, extent, split, smallest, high):
    loudness, own = 1.0, jax.random.fold_in(rng, 6)
    for dim, shards_of in split:
        draws = jnp.exp(jax.random.uniform(jax.random.fold_in(own, dim), (shards_of,), jnp.float32, smallest / len(split), high / len(split)))
        loudness = loudness * jnp.repeat(draws, extent[dim] // shards_of).reshape([-1 if axis == dim else 1 for axis in range(len(extent))])
    return loudness


def bell_draw(key, shape, width, bound, cuts=(), kind=jnp.bfloat16):
    level = levels(key, shape, cuts, -0.22, 0.18) if cuts else 1.0
    drawn = jax.random.normal(key, shape, jnp.float32) * width * level
    return jnp.minimum(jnp.maximum(drawn, -bound), bound).astype(kind)


def setup_inputs(seed: int = 0) -> dict:
    seeds = jax.random.split(jax.random.key(seed), 7)
    features = bell_draw(seeds[0], (NODES, F), 1.0, 6.0, ((0, 8), (1, 4)))
    weight = bell_draw(seeds[1], (F, F), F ** -0.5, 0.375)
    cotangent = bell_draw(seeds[2], (NODES, F), 1.0, 6.0, ((0, 32),))
    block_values = bell_draw(seeds[3], (ROW_TILES, COL_TILES, NNZB, 128, 128), (16384 * NNZB // NODE_DEV) ** -0.5, 0.0625, ((0, 4), (1, 8)))
    block_coords = draw_block_coords(jax.random.fold_in(seeds[6], 71), 0)
    block_counts = draw_block_counts(jax.random.fold_in(seeds[6], 71), 0)
    return {"features": features, "weight": weight, "cotangent": cotangent, "block_values": block_values, "block_coords": block_coords, "block_counts": block_counts}


def reference(features, weight, cotangent, block_values, block_coords, block_counts):
    tiles_total = ROW_TILES * COL_TILES
    blocks = block_values.reshape(tiles_total, NNZB, 128, 128)
    coords = block_coords.reshape(tiles_total, NNZB, 2)
    counts = block_counts.reshape(tiles_total)
    tile_ids = jnp.arange(tiles_total, dtype=jnp.int32)
    slot_ids = jnp.arange(NNZB, dtype=jnp.int32)
    feat_blocks = features.reshape(NODES // 128, 128, F)

    def places(coords_t, tile):
        tile_row = tile // COL_TILES
        tile_col = tile % COL_TILES
        rows_at = (tile_row * TILE_RB + coords_t[:, 0]).astype(jnp.int32)
        cols_at = (tile_col * TILE_CB + coords_t[:, 1]).astype(jnp.int32)
        return rows_at, cols_at

    def forward_step(total, inputs):
        blocks_t, coords_t, count_t, tile = inputs
        rows_at, cols_at = places(coords_t, tile)
        chosen = feat_blocks[cols_at].astype(jnp.float32)
        product = jnp.einsum("bij,bjf->bif", blocks_t.astype(jnp.float32), chosen,
                             precision=lax.Precision.HIGHEST)
        is_live = (slot_ids < count_t).astype(jnp.float32)
        return total.at[rows_at].add(product * is_live[:, None, None]), None

    start = jnp.zeros((NODES // 128, 128, F), jnp.float32)
    total, _ = lax.scan(forward_step, start, (blocks, coords, counts, tile_ids))
    aggregate = total.reshape(NODES, F).astype(jnp.bfloat16)
    pre_act = jnp.dot(aggregate, weight, preferred_element_type=jnp.float32)
    sigma = jax.nn.sigmoid(pre_act)
    activations = (pre_act * sigma).astype(jnp.bfloat16)
    grad_pre = (cotangent.astype(jnp.float32) * sigma * (1.0 + pre_act * (1.0 - sigma))).astype(jnp.bfloat16)
    weight_grad = jnp.dot(aggregate.T, grad_pre, preferred_element_type=jnp.float32)
    back_rows = jnp.dot(grad_pre, weight.T, preferred_element_type=jnp.float32).astype(jnp.bfloat16)
    back_blocks = back_rows.reshape(NODES // 128, 128, F)

    def backward_step(total, inputs):
        blocks_t, coords_t, count_t, tile = inputs
        rows_at, cols_at = places(coords_t, tile)
        chosen = back_blocks[rows_at].astype(jnp.float32)
        product = jnp.einsum("bji,bjf->bif", blocks_t.astype(jnp.float32), chosen,
                             precision=lax.Precision.HIGHEST)
        is_live = (slot_ids < count_t).astype(jnp.float32)
        return total.at[cols_at].add(product * is_live[:, None, None]), None

    total_back, _ = lax.scan(backward_step, start, (blocks, coords, counts, tile_ids))
    input_grad = total_back.reshape(NODES, F).astype(jnp.bfloat16)
    return (activations, input_grad, weight_grad)
```

```python
import functools
import math

import jax
import jax.numpy as jnp
from jax import lax
from jax.experimental import pallas as pl
from jax.experimental.pallas import tpu as pltpu
from jax.sharding import PartitionSpec as P


def local_xla(features, weight, cotangent, block_values, block_coords, block_counts):
    blocks = block_values[0, 0]
    coords = block_coords[0, 0]
    live_count = block_counts[0, 0]
    slots = blocks.shape[0]
    gathered = lax.all_gather(features, "row", axis=1, tiled=True)
    feat_width = gathered.shape[1]
    col_blocks = gathered.shape[0] // 128
    row_blocks = cotangent.shape[0] * lax.axis_size(("col", "rep")) // 128
    feat_blocks = gathered.reshape(col_blocks, 128, feat_width)
    is_live = (jnp.arange(slots, dtype=jnp.int32) < live_count).astype(jnp.float32)
    per_turn = math.gcd(slots, 64)
    rounds = slots // per_turn
    pieces = (
        blocks.reshape(rounds, per_turn, 128, 128),
        coords[:, 0].reshape(rounds, per_turn),
        coords[:, 1].reshape(rounds, per_turn),
        is_live.reshape(rounds, per_turn),
    )

    def forward_step(total, piece):
        blocks_g, rows_g, cols_g, live_g = piece
        chosen = feat_blocks[cols_g]
        product = jnp.einsum("bij,bjf->bif", blocks_g, chosen, preferred_element_type=jnp.float32)
        return (total.at[rows_g].add(product * live_g[:, None, None]), None)

    partial_value, _ = lax.scan(
        forward_step, jnp.zeros((row_blocks, 128, feat_width), jnp.float32), pieces
    )
    partial_value = partial_value.reshape(row_blocks * 128, feat_width)
    summed = lax.psum_scatter(partial_value, ("col", "rep"), scatter_dimension=0, tiled=True)
    aggregate = summed.astype(jnp.bfloat16)
    pre_act = jnp.dot(aggregate, weight, preferred_element_type=jnp.float32)
    sigma = jax.nn.sigmoid(pre_act)
    activations = (pre_act * sigma).astype(jnp.bfloat16)
    grad_pre = (cotangent.astype(jnp.float32) * sigma * (1.0 + pre_act * (1.0 - sigma))).astype(
        jnp.bfloat16
    )
    weight_terms = jnp.dot(aggregate.T, grad_pre, preferred_element_type=jnp.float32)
    share = lax.psum_scatter(
        weight_terms.astype(jnp.bfloat16), ("col", "rep"), scatter_dimension=0, tiled=True
    ).astype(jnp.float32)
    share = lax.psum(share, "row")
    weight_grad = lax.all_gather(share, ("col", "rep"), axis=0, tiled=True)
    back_rows = jnp.dot(grad_pre, weight.T, preferred_element_type=jnp.float32).astype(jnp.bfloat16)
    back_all = lax.all_gather(back_rows, ("col", "rep"), axis=0, tiled=True)
    back_blocks = back_all.reshape(row_blocks, 128, back_all.shape[1])

    def backward_step(total, piece):
        blocks_g, rows_g, cols_g, live_g = piece
        chosen = back_blocks[rows_g]
        product = jnp.einsum("bji,bjf->bif", blocks_g, chosen, preferred_element_type=jnp.float32)
        return (total.at[cols_g].add(product * live_g[:, None, None]), None)

    grad_terms, _ = lax.scan(
        backward_step, jnp.zeros((col_blocks, 128, back_all.shape[1]), jnp.float32), pieces
    )
    grad_terms = grad_terms.reshape(col_blocks * 128, back_all.shape[1])
    input_grad = lax.psum_scatter(
        grad_terms.astype(jnp.bfloat16), "row", scatter_dimension=1, tiled=True
    )
    return (activations, input_grad, weight_grad)


BF16 = jnp.bfloat16
F32 = jnp.float32
VMEM_BUDGET = 60 * 2**20
MESH = pl.DeviceIdType.MESH


def dot(a, b, ca=1, cb=0):
    return lax.dot_general(a, b, (((ca,), (cb,)), ((), ())), preferred_element_type=F32)


def layer_kernel(
    sizes,
    table,
    feat_in,
    weight_in,
    cot_in,
    blocks_hbm,
    act_out,
    igrad_out,
    wgrad_out,
    fbuf,
    bbuf,
    sums,
    dense,
    feat,
    pbuf,
    prec,
    qbuf,
    qrec,
    own_back,
    brec,
    bpar,
    total,
    zbuf,
    zrec,
    wbuf,
    wrec,
    shard_buf,
    srec,
    wall,
    wgather,
    load_sem,
    f_sem,
    p_sem,
    q_sem,
    b_sem,
    c_sem,
    z_sem,
    w_sem,
    s_sem,
    g_sem,
    h_sem,
):
    nrow, ncol, nrep = sizes
    nh = nrep // 2
    group = ncol * nrep
    slots = bbuf.shape[0]
    nodes, width = act_out.shape
    fw = feat_in.shape[1]
    col_nodes = feat_in.shape[0]
    row_blocks, col_blocks = dense.shape[0] // 128, dense.shape[1] // 128
    r, c, p = lax.axis_index("row"), lax.axis_index("col"), lax.axis_index("rep")
    h, k = p // 2, p % 2
    g = c * nrep + p
    partner = h * 2 + (1 - k)
    offsets = [(dc, dh) for dc in reversed(range(ncol)) for dh in reversed(range(nh))]
    chips = len(offsets)

    def to_row(j):
        return {"row": (r + j) % nrow}

    def to_group(j):
        q = (g + j) % group
        return {"col": q // nrep, "rep": q % nrep}

    def to_chip(i):
        dc, dh = offsets[i]
        return {"col": (c + dc) % ncol, "rep": ((h + dh) % nh) * 2 + k}

    def part_to(i, core):
        dc, dh = offsets[i]
        return ((c + dc) % ncol) * nrep + ((h + dh) % nh) * 2 + core

    def part_from(i, core):
        dc, dh = offsets[i]
        return ((c + ncol - dc) % ncol) * nrep + ((h + nh - dh) % nh) * 2 + core

    def rcopy(src, dst, sems, i, device):
        return pltpu.make_async_remote_copy(
            src_ref=src,
            dst_ref=dst,
            send_sem=sems.at[0, i],
            recv_sem=sems.at[1, i],
            device_id=device,
            device_id_type=MESH,
        )

    chunks = load_sem.shape[0]
    per = slots // chunks
    loads = []
    for i in range(chunks):
        span = pl.ds(i * per, per)
        loads.append(pltpu.make_async_copy(blocks_hbm.at[span], bbuf.at[span], load_sem.at[i]))
        loads[-1].start()

    barrier = pltpu.get_barrier_semaphore()
    for j in range(1, nrow):
        pl.semaphore_signal(barrier, inc=1, device_id=to_row(j), device_id_type=MESH)
    for j in range(1, group):
        pl.semaphore_signal(barrier, inc=1, device_id=to_group(j), device_id_type=MESH)

    packs = 128 // fw
    piece = col_nodes // packs
    packed = jnp.concatenate(
        [feat_in[i * piece : (i + 1) * piece, :] for i in range(packs)], axis=1
    )
    fbuf[r] = packed
    pl.semaphore_wait(barrier, nrow - 1 + group - 1)
    fcopies = []
    for j in range(1, nrow):
        fcopies.append(rcopy(fbuf.at[r], fbuf.at[r], f_sem, j - 1, to_row(j)))
        fcopies[-1].start()

    sums[0] = jnp.zeros((128, 128), F32)
    for i in range(chunks):
        loads[i].wait()

        def add_slot(s, carry):
            sums[s + 1] = sums[table[s]] + bbuf[s].astype(F32)
            return carry

        lax.fori_loop(i * per, (i + 1) * per, add_slot, 0)

    def fill(rb, carry):
        for cb in range(col_blocks):
            block = sums[table[slots + rb * col_blocks + cb]]
            dense[pl.ds(rb * 128, 128), cb * 128 : (cb + 1) * 128] = block.astype(BF16)
        return carry

    lax.fori_loop(0, row_blocks, fill, 0)

    for copy in fcopies:
        copy.wait()
    for q in range(packs):
        for m in range(width // 128):
            feat[q * piece : (q + 1) * piece, m * 128 : (m + 1) * 128] = jnp.concatenate(
                [fbuf[m * packs + e, :, q * fw : (q + 1) * fw] for e in range(packs)], axis=1
            )

    def partial(part):
        return dot(dense[pl.ds(part * nodes, nodes), :], feat[...])

    pcopies = []
    for i in range(chips):
        pbuf[i] = partial(part_to(i, 1 - k)).astype(BF16)
        pcopies.append(rcopy(pbuf.at[i], prec.at[i], p_sem, i, {"rep": partner}))
        pcopies[i].start()
    qcopies = []
    for i in range(chips - 1):
        mine = partial(part_to(i, k))
        pcopies[i].wait()
        qbuf[i] = (mine + prec[i].astype(F32)).astype(BF16)
        qcopies.append(rcopy(qbuf.at[i], qrec.at[i], q_sem, i, to_chip(i)))
        qcopies[i].start()
    summed = partial(g)
    pcopies[chips - 1].wait()
    summed = summed + prec[chips - 1].astype(F32)
    for i in reversed(range(chips - 1)):
        qcopies[i].wait()
        summed = summed + qrec[i].astype(F32)

    aggregate = summed.astype(BF16)
    pre_act = dot(aggregate, weight_in[...])
    sigma = jax.nn.sigmoid(pre_act)
    grad_pre = (cot_in[...].astype(F32) * sigma * (1.0 + pre_act * (1.0 - sigma))).astype(BF16)
    own_back[...] = dot(weight_in[...], grad_pre, 1, 1).astype(BF16)
    bcopies, ccopies = [], []
    for i in range(chips - 1):
        bcopies.append(rcopy(own_back, brec.at[i], b_sem, i, to_chip(i)))
        bcopies[i].start()
    first = rcopy(own_back, bpar.at[chips - 1], c_sem, chips - 1, {"rep": partner})
    first.start()

    terms = dot(aggregate, grad_pre, 0, 0)
    wrows = width // nrow
    wbuf[...] = terms.astype(BF16).reshape(nrow, wrows, width)
    wcopies = []
    for j in range(1, nrow):
        wcopies.append(rcopy(wbuf.at[(r + j) % nrow], wrec.at[j - 1], w_sem, j - 1, to_row(j)))
        wcopies[-1].start()
    act_out[...] = (pre_act * sigma).astype(BF16)

    def back_term(piece_t, part):
        return dot(piece_t, dense[pl.ds(part * nodes, nodes), :])

    total[...] = back_term(own_back[...], g)
    first.wait()
    total[...] += back_term(bpar[chips - 1], c * nrep + partner)

    for copy in wcopies:
        copy.wait()
    share = wbuf[r].astype(F32)
    for j in range(nrow - 1):
        share = share + wrec[j].astype(F32)
    srows = wrows // group
    shard_buf[...] = share.reshape(group, srows, width)
    scopies = []
    for j in range(1, group):
        scopies.append(rcopy(shard_buf.at[(g + j) % group], srec.at[j - 1], s_sem, j - 1, to_group(j)))
        scopies[-1].start()

    for i in reversed(range(chips - 1)):
        bcopies[i].wait()
        ccopies.append(rcopy(brec.at[i], bpar.at[i], c_sem, i, {"rep": partner}))
        ccopies[-1].start()
        total[...] += back_term(brec[i], part_from(i, k))

    for copy in scopies:
        copy.wait()
    final = shard_buf[g]
    for j in range(group - 1):
        final = final + srec[j]
    wall[g] = final
    gcopies = []
    for j in range(1, group):
        gcopies.append(rcopy(wall.at[g], wall.at[g], g_sem, j - 1, to_group(j)))
        gcopies[-1].start()

    for n, i in enumerate(reversed(range(chips - 1))):
        ccopies[n].wait()
        total[...] += back_term(bpar[i], part_from(i, 1 - k))

    zcopies = []
    for j in range(1, nrow):
        q = (r + j) % nrow
        zbuf[j - 1] = total[pl.ds(q * fw, fw), :].astype(BF16)
        zcopies.append(rcopy(zbuf.at[j - 1], zrec.at[j - 1], z_sem, j - 1, to_row(j)))
        zcopies[-1].start()

    for copy in gcopies:
        copy.wait()
    wgather[r] = wall[...].reshape(wrows, width)
    hcopies = []
    for j in range(1, nrow):
        hcopies.append(rcopy(wgather.at[r], wgather.at[r], h_sem, j - 1, to_row(j)))
        hcopies[-1].start()

    mine = total[pl.ds(r * fw, fw), :]
    for j in range(nrow - 1):
        zcopies[j].wait()
        mine = mine + zrec[j].astype(F32)
    stacked = jnp.concatenate(
        [mine[:, i * piece : (i + 1) * piece] for i in range(packs)], axis=0
    ).T
    for i in range(packs):
        igrad_out[i * piece : (i + 1) * piece, :] = stacked[:, i * fw : (i + 1) * fw].astype(BF16)
    for copy in hcopies:
        copy.wait()
    wgrad_out[...] = wgather[...].reshape(width, width)


def local_kernel(sizes, features, weight, cotangent, block_values, block_coords, block_counts):
    nrow, ncol, nrep = sizes
    group = ncol * nrep
    chips = group // 2
    blocks = block_values[0, 0]
    coords = block_coords[0, 0]
    live_count = block_counts[0, 0]
    slots = blocks.shape[0]
    nodes, width = cotangent.shape
    col_nodes, fw = features.shape
    row_blocks, col_blocks = nodes * group // 128, col_nodes // 128
    places = row_blocks * col_blocks
    place = coords[:, 0] * col_blocks + coords[:, 1]
    slot = jnp.arange(slots, dtype=jnp.int32)
    wanted = jnp.concatenate([place, jnp.arange(places, dtype=jnp.int32)])
    limit = jnp.concatenate([slot, jnp.full((places,), slots, jnp.int32)])
    hit = (wanted[:, None] == place[None, :]) & (
        slot[None, :] < jnp.minimum(limit, live_count)[:, None]
    )
    table = jnp.max(jnp.where(hit, slot[None, :] + 1, 0), axis=1)

    packs = 128 // fw
    chunks = math.gcd(slots, 8)
    wrows = width // nrow
    srows = wrows // group
    square = (nodes, width)
    vmem = functools.partial(pl.BlockSpec, memory_space=pltpu.VMEM)
    dma = pltpu.SemaphoreType.DMA
    return pl.pallas_call(
        functools.partial(layer_kernel, sizes),
        out_shape=(
            jax.ShapeDtypeStruct(square, BF16),
            jax.ShapeDtypeStruct((col_nodes, fw), BF16),
            jax.ShapeDtypeStruct((width, width), F32),
        ),
        in_specs=[
            pl.BlockSpec(memory_space=pltpu.SMEM),
            vmem(),
            vmem(),
            vmem(),
            pl.BlockSpec(memory_space=pl.ANY),
        ],
        out_specs=(vmem(), vmem(), vmem()),
        scratch_shapes=[
            pltpu.VMEM((nrow, col_nodes // packs, 128), BF16),
            pltpu.VMEM((slots, 128, 128), BF16),
            pltpu.VMEM((slots + 1, 128, 128), F32),
            pltpu.VMEM((row_blocks * 128, col_nodes), BF16),
            pltpu.VMEM((col_nodes, width), BF16),
            pltpu.VMEM((chips,) + square, BF16),
            pltpu.VMEM((chips,) + square, BF16),
            pltpu.VMEM((chips - 1,) + square, BF16),
            pltpu.VMEM((chips - 1,) + square, BF16),
            pltpu.VMEM((width, nodes), BF16),
            pltpu.VMEM((chips - 1, width, nodes), BF16),
            pltpu.VMEM((chips, width, nodes), BF16),
            pltpu.VMEM((width, col_nodes), F32),
            pltpu.VMEM((nrow - 1, fw, col_nodes), BF16),
            pltpu.VMEM((nrow - 1, fw, col_nodes), BF16),
            pltpu.VMEM((nrow, wrows, width), BF16),
            pltpu.VMEM((nrow - 1, wrows, width), BF16),
            pltpu.VMEM((group, srows, width), F32),
            pltpu.VMEM((group - 1, srows, width), F32),
            pltpu.VMEM((group, srows, width), F32),
            pltpu.VMEM((nrow, wrows, width), F32),
            dma((chunks,)),
            dma((2, nrow - 1)),
            dma((2, chips)),
            dma((2, chips - 1)),
            dma((2, chips - 1)),
            dma((2, chips)),
            dma((2, nrow - 1)),
            dma((2, nrow - 1)),
            dma((2, group - 1)),
            dma((2, group - 1)),
            dma((2, nrow - 1)),
        ],
        compiler_params=pltpu.CompilerParams(
            collective_id=0, has_side_effects=True, vmem_limit_bytes=VMEM_BUDGET
        ),
    )(table, features, weight, cotangent, blocks)


def fits(mesh, features, weight, cotangent, block_values):
    nrow, ncol, nrep = (mesh.shape[name] for name in ("row", "col", "rep"))
    group = ncol * nrep
    width = features.shape[1]
    fw = width // nrow
    rows, cols = cotangent.shape[0] // nrow, features.shape[0] // group
    tile = rows * cols * 2 + block_values.shape[2] * 128 * 128 * 6
    moved = 8 * rows * width + 12 * cols * width
    whole = nrep % 2 == 0 and 128 % fw == 0 and (width // nrow) % (8 * group) == 0
    return whole and nrow > 1 and group > 2 and tile + moved < VMEM_BUDGET * 3 // 4


def solution(mesh):
    in_specs = (
        P(("col", "rep"), "row"),
        P(),
        P(("row", "col", "rep"), None),
        P("row", ("col", "rep"), None, None, None),
        P("row", ("col", "rep"), None, None),
        P("row", ("col", "rep")),
    )
    out_specs = (P(("row", "col", "rep"), None), P(("col", "rep"), "row"), P())
    sizes = tuple(mesh.shape[name] for name in ("row", "col", "rep"))

    def run(features, weight, cotangent, block_values, block_coords, block_counts):
        if fits(mesh, features, weight, cotangent, block_values):
            body = functools.partial(local_kernel, sizes)
        else:
            body = local_xla
        return jax.shard_map(
            body, mesh=mesh, in_specs=in_specs, out_specs=out_specs, check_vma=False
        )(features, weight, cotangent, block_values, block_coords, block_counts)

    return run
```

```python
import functools
import math

import jax
import jax.numpy as jnp
from jax import lax
from jax.experimental import pallas as pl
from jax.experimental.pallas import tpu as pltpu
from jax.sharding import PartitionSpec as P


def local_xla(features, weight, cotangent, block_values, block_coords, block_counts):
    blocks = block_values[0, 0]
    coords = block_coords[0, 0]
    live_count = block_counts[0, 0]
    slots = blocks.shape[0]
    gathered = lax.all_gather(features, "row", axis=1, tiled=True)
    feat_width = gathered.shape[1]
    col_blocks = gathered.shape[0] // 128
    row_blocks = cotangent.shape[0] * lax.axis_size(("col", "rep")) // 128
    feat_blocks = gathered.reshape(col_blocks, 128, feat_width)
    is_live = (jnp.arange(slots, dtype=jnp.int32) < live_count).astype(jnp.float32)
    per_turn = math.gcd(slots, 64)
    rounds = slots // per_turn
    pieces = (
        blocks.reshape(rounds, per_turn, 128, 128),
        coords[:, 0].reshape(rounds, per_turn),
        coords[:, 1].reshape(rounds, per_turn),
        is_live.reshape(rounds, per_turn),
    )

    def forward_step(total, piece):
        blocks_g, rows_g, cols_g, live_g = piece
        chosen = feat_blocks[cols_g]
        product = jnp.einsum("bij,bjf->bif", blocks_g, chosen, preferred_element_type=jnp.float32)
        return (total.at[rows_g].add(product * live_g[:, None, None]), None)

    partial_value, _ = lax.scan(
        forward_step, jnp.zeros((row_blocks, 128, feat_width), jnp.float32), pieces
    )
    partial_value = partial_value.reshape(row_blocks * 128, feat_width)
    summed = lax.psum_scatter(partial_value, ("col", "rep"), scatter_dimension=0, tiled=True)
    aggregate = summed.astype(jnp.bfloat16)
    pre_act = jnp.dot(aggregate, weight, preferred_element_type=jnp.float32)
    sigma = jax.nn.sigmoid(pre_act)
    activations = (pre_act * sigma).astype(jnp.bfloat16)
    grad_pre = (cotangent.astype(jnp.float32) * sigma * (1.0 + pre_act * (1.0 - sigma))).astype(
        jnp.bfloat16
    )
    weight_terms = jnp.dot(aggregate.T, grad_pre, preferred_element_type=jnp.float32)
    share = lax.psum_scatter(
        weight_terms.astype(jnp.bfloat16), ("col", "rep"), scatter_dimension=0, tiled=True
    ).astype(jnp.float32)
    share = lax.psum(share, "row")
    weight_grad = lax.all_gather(share, ("col", "rep"), axis=0, tiled=True)
    back_rows = jnp.dot(grad_pre, weight.T, preferred_element_type=jnp.float32).astype(jnp.bfloat16)
    back_all = lax.all_gather(back_rows, ("col", "rep"), axis=0, tiled=True)
    back_blocks = back_all.reshape(row_blocks, 128, back_all.shape[1])

    def backward_step(total, piece):
        blocks_g, rows_g, cols_g, live_g = piece
        chosen = back_blocks[rows_g]
        product = jnp.einsum("bji,bjf->bif", blocks_g, chosen, preferred_element_type=jnp.float32)
        return (total.at[cols_g].add(product * live_g[:, None, None]), None)

    grad_terms, _ = lax.scan(
        backward_step, jnp.zeros((col_blocks, 128, back_all.shape[1]), jnp.float32), pieces
    )
    grad_terms = grad_terms.reshape(col_blocks * 128, back_all.shape[1])
    input_grad = lax.psum_scatter(
        grad_terms.astype(jnp.bfloat16), "row", scatter_dimension=1, tiled=True
    )
    return (activations, input_grad, weight_grad)


BF16 = jnp.bfloat16
F32 = jnp.float32
VMEM_BUDGET = 60 * 2**20
MESH = pl.DeviceIdType.MESH


def dot(a, b, ca=1, cb=0):
    return lax.dot_general(a, b, (((ca,), (cb,)), ((), ())), preferred_element_type=F32)


def layer_kernel(
    sizes,
    count_in,
    coords_in,
    feat_in,
    weight_in,
    cot_in,
    blocks_hbm,
    act_out,
    igrad_out,
    wgrad_out,
    fbuf,
    bbuf,
    sums,
    dense,
    feat,
    pbuf,
    prec,
    qbuf,
    qrec,
    own_back,
    brec,
    bpar,
    total,
    zbuf,
    zrec,
    wbuf,
    wrec,
    shard_buf,
    srec,
    wall,
    wgather,
    tvec,
    table,
    load_sem,
    t_sem,
    f_sem,
    p_sem,
    q_sem,
    b_sem,
    c_sem,
    z_sem,
    w_sem,
    s_sem,
    g_sem,
    h_sem,
):
    nrow, ncol, nrep = sizes
    nh = nrep // 2
    group = ncol * nrep
    slots = bbuf.shape[0]
    nodes, width = act_out.shape
    fw, col_nodes = feat_in.shape
    row_blocks, col_blocks = dense.shape[0] // 128, dense.shape[1] // 128
    r, c, p = lax.axis_index("row"), lax.axis_index("col"), lax.axis_index("rep")
    h, k = p // 2, p % 2
    g = c * nrep + p
    partner = h * 2 + (1 - k)
    offsets = [(dc, dh) for dc in reversed(range(ncol)) for dh in reversed(range(nh))]
    chips = len(offsets)

    def to_row(j):
        return {"row": (r + j) % nrow}

    def to_group(j):
        q = (g + j) % group
        return {"col": q // nrep, "rep": q % nrep}

    def to_chip(i):
        dc, dh = offsets[i]
        return {"col": (c + dc) % ncol, "rep": ((h + dh) % nh) * 2 + k}

    def part_to(i, core):
        dc, dh = offsets[i]
        return ((c + dc) % ncol) * nrep + ((h + dh) % nh) * 2 + core

    def part_from(i, core):
        dc, dh = offsets[i]
        return ((c + ncol - dc) % ncol) * nrep + ((h + nh - dh) % nh) * 2 + core

    def rcopy(src, dst, sems, i, device):
        return pltpu.make_async_remote_copy(
            src_ref=src,
            dst_ref=dst,
            send_sem=sems.at[0, i],
            recv_sem=sems.at[1, i],
            device_id=device,
            device_id_type=MESH,
        )

    chunks = load_sem.shape[0]
    per = slots // chunks
    loads = []
    for i in range(chunks):
        span = pl.ds(i * per, per)
        loads.append(pltpu.make_async_copy(blocks_hbm.at[span], bbuf.at[span], load_sem.at[i]))
        loads[-1].start()

    barrier = pltpu.get_barrier_semaphore()
    for j in range(1, nrow):
        pl.semaphore_signal(barrier, inc=1, device_id=to_row(j), device_id_type=MESH)
    for j in range(1, group):
        pl.semaphore_signal(barrier, inc=1, device_id=to_group(j), device_id_type=MESH)

    pl.semaphore_wait(barrier, nrow - 1 + group - 1)
    fcopies = []
    for j in range(1, nrow):
        fcopies.append(rcopy(feat_in, fbuf.at[r], f_sem, j - 1, to_row(j)))
        fcopies[-1].start()

    fbuf[r] = feat_in[...]

    places = row_blocks * col_blocks
    live = count_in[0, 0]
    row_form = coords_in[0:1, :] * col_blocks + coords_in[1:2, :]
    column_form = jnp.broadcast_to(row_form, (slots, slots)).T
    mine_at = lax.broadcasted_iota(jnp.int32, (slots, slots), 0)
    other_at = lax.broadcasted_iota(jnp.int32, (slots, slots), 1)
    hit = (column_form == row_form) & (mine_at < jnp.minimum(other_at, live))
    tvec[0:1, 0:slots] = jnp.max(jnp.where(hit, mine_at + 1, 0), axis=0, keepdims=True)
    for start in range(0, places, slots):
        hit = (column_form == other_at + start) & (mine_at < live)
        tvec[0:1, slots + start : 2 * slots + start] = jnp.max(
            jnp.where(hit, mine_at + 1, 0), axis=0, keepdims=True
        )
    tcopy = pltpu.make_async_copy(tvec, table, t_sem)
    tcopy.start()
    tcopy.wait()

    sums[0] = jnp.zeros((128, 128), F32)
    for i in range(chunks):
        loads[i].wait()

        def add_slot(s, carry):
            sums[s + 1] = sums[table[0, s]] + bbuf[s].astype(F32)
            return carry

        lax.fori_loop(i * per, (i + 1) * per, add_slot, 0)

    def fill(rb, carry):
        for cb in range(col_blocks):
            block = sums[table[0, slots + rb * col_blocks + cb]]
            dense[pl.ds(rb * 128, 128), cb * 128 : (cb + 1) * 128] = block.astype(BF16)
        return carry

    lax.fori_loop(0, row_blocks, fill, 0)

    for copy in fcopies:
        copy.wait()
    feat[...] = fbuf[...].reshape(width, col_nodes).T

    def partial(part):
        return dot(dense[pl.ds(part * nodes, nodes), :], feat[...])

    pcopies = []
    for i in range(chips):
        pbuf[i] = partial(part_to(i, 1 - k)).astype(BF16)
        pcopies.append(rcopy(pbuf.at[i], prec.at[i], p_sem, i, {"rep": partner}))
        pcopies[i].start()
    qcopies = []
    for i in range(chips - 1):
        mine = partial(part_to(i, k))
        pcopies[i].wait()
        qbuf[i] = (mine + prec[i].astype(F32)).astype(BF16)
        qcopies.append(rcopy(qbuf.at[i], qrec.at[i], q_sem, i, to_chip(i)))
        qcopies[i].start()
    summed = partial(g)
    pcopies[chips - 1].wait()
    summed = summed + prec[chips - 1].astype(F32)
    for i in reversed(range(chips - 1)):
        qcopies[i].wait()
        summed = summed + qrec[i].astype(F32)

    aggregate = summed.astype(BF16)
    pre_act = dot(aggregate, weight_in[...])
    sigma = jax.nn.sigmoid(pre_act)
    grad_pre = (cot_in[...].astype(F32) * sigma * (1.0 + pre_act * (1.0 - sigma))).astype(BF16)
    own_back[...] = dot(weight_in[...], grad_pre, 1, 1).astype(BF16)
    bcopies, ccopies = [], []
    for i in range(chips - 1):
        bcopies.append(rcopy(own_back, brec.at[i], b_sem, i, to_chip(i)))
        bcopies[i].start()
    first = rcopy(own_back, bpar.at[chips - 1], c_sem, chips - 1, {"rep": partner})
    first.start()

    terms = dot(aggregate, grad_pre, 0, 0)
    wrows = width // nrow
    wbuf[...] = terms.astype(BF16).reshape(nrow, wrows, width)
    wcopies = []
    for j in range(1, nrow):
        wcopies.append(rcopy(wbuf.at[(r + j) % nrow], wrec.at[j - 1], w_sem, j - 1, to_row(j)))
        wcopies[-1].start()
    act_out[...] = (pre_act * sigma).astype(BF16)

    def back_term(piece_t, part):
        return dot(piece_t, dense[pl.ds(part * nodes, nodes), :])

    total[...] = back_term(own_back[...], g)
    first.wait()
    total[...] += back_term(bpar[chips - 1], c * nrep + partner)

    for copy in wcopies:
        copy.wait()
    share = wbuf[r].astype(F32)
    for j in range(nrow - 1):
        share = share + wrec[j].astype(F32)
    srows = wrows // group
    shard_buf[...] = share.reshape(group, srows, width)
    scopies = []
    for j in range(1, group):
        scopies.append(rcopy(shard_buf.at[(g + j) % group], srec.at[j - 1], s_sem, j - 1, to_group(j)))
        scopies[-1].start()

    for i in reversed(range(chips - 1)):
        bcopies[i].wait()
        ccopies.append(rcopy(brec.at[i], bpar.at[i], c_sem, i, {"rep": partner}))
        ccopies[-1].start()
        total[...] += back_term(brec[i], part_from(i, k))

    for copy in scopies:
        copy.wait()
    final = shard_buf[g]
    for j in range(group - 1):
        final = final + srec[j]
    wall[g] = final
    gcopies = []
    for j in range(1, group):
        gcopies.append(rcopy(wall.at[g], wall.at[g], g_sem, j - 1, to_group(j)))
        gcopies[-1].start()

    for n, i in enumerate(reversed(range(chips - 1))):
        ccopies[n].wait()
        total[...] += back_term(bpar[i], part_from(i, 1 - k))

    zcopies = []
    for j in range(1, nrow):
        q = (r + j) % nrow
        zbuf[j - 1] = total[pl.ds(q * fw, fw), :].astype(BF16)
        zcopies.append(rcopy(zbuf.at[j - 1], zrec.at[j - 1], z_sem, j - 1, to_row(j)))
        zcopies[-1].start()

    for copy in gcopies:
        copy.wait()
    wgather[r] = wall[...].reshape(wrows, width)
    hcopies = []
    for j in range(1, nrow):
        hcopies.append(rcopy(wgather.at[r], wgather.at[r], h_sem, j - 1, to_row(j)))
        hcopies[-1].start()

    mine = total[pl.ds(r * fw, fw), :]
    for j in range(nrow - 1):
        zcopies[j].wait()
        mine = mine + zrec[j].astype(F32)
    igrad_out[...] = mine.astype(BF16)
    for copy in hcopies:
        copy.wait()
    wgrad_out[...] = wgather[...].reshape(width, width)


def keep_kernel(a_in, b_in, c_in, a_out, b_out, c_out):
    a_out[...] = a_in[...]
    b_out[...] = b_in[...]
    c_out[...] = c_in[...]


def local_kernel(sizes, features, weight, cotangent, block_values, block_coords, block_counts):
    nrow, ncol, nrep = sizes
    group = ncol * nrep
    chips = group // 2
    blocks = block_values[0, 0]
    slots = blocks.shape[0]
    nodes, width = cotangent.shape
    col_nodes, fw = features.shape
    row_blocks = nodes * group // 128
    places = row_blocks * (col_nodes // 128)
    chunks = math.gcd(slots, 8)
    wrows = width // nrow
    srows = wrows // group
    square = (nodes, width)
    vmem = functools.partial(pl.BlockSpec, memory_space=pltpu.VMEM)
    dma = pltpu.SemaphoreType.DMA
    outs = pl.pallas_call(
        functools.partial(layer_kernel, sizes),
        out_shape=(
            jax.ShapeDtypeStruct(square, BF16),
            jax.ShapeDtypeStruct((fw, col_nodes), BF16),
            jax.ShapeDtypeStruct((width, width), F32),
        ),
        in_specs=[
            pl.BlockSpec(memory_space=pltpu.SMEM),
            vmem(),
            vmem(),
            vmem(),
            vmem(),
            pl.BlockSpec(memory_space=pl.ANY),
        ],
        out_specs=(vmem(), vmem(), vmem()),
        scratch_shapes=[
            pltpu.VMEM((nrow, fw, col_nodes), BF16),
            pltpu.VMEM((slots, 128, 128), BF16),
            pltpu.VMEM((slots + 1, 128, 128), F32),
            pltpu.VMEM((row_blocks * 128, col_nodes), BF16),
            pltpu.VMEM((col_nodes, width), BF16),
            pltpu.VMEM((chips,) + square, BF16),
            pltpu.VMEM((chips,) + square, BF16),
            pltpu.VMEM((chips - 1,) + square, BF16),
            pltpu.VMEM((chips - 1,) + square, BF16),
            pltpu.VMEM((width, nodes), BF16),
            pltpu.VMEM((chips - 1, width, nodes), BF16),
            pltpu.VMEM((chips, width, nodes), BF16),
            pltpu.VMEM((width, col_nodes), F32),
            pltpu.VMEM((nrow - 1, fw, col_nodes), BF16),
            pltpu.VMEM((nrow - 1, fw, col_nodes), BF16),
            pltpu.VMEM((nrow, wrows, width), BF16),
            pltpu.VMEM((nrow - 1, wrows, width), BF16),
            pltpu.VMEM((group, srows, width), F32),
            pltpu.VMEM((group - 1, srows, width), F32),
            pltpu.VMEM((group, srows, width), F32),
            pltpu.VMEM((nrow, wrows, width), F32),
            pltpu.VMEM((1, slots + places), jnp.int32),
            pltpu.SMEM((1, slots + places), jnp.int32),
            dma((chunks,)),
            dma,
            dma((2, nrow - 1)),
            dma((2, chips)),
            dma((2, chips - 1)),
            dma((2, chips - 1)),
            dma((2, chips)),
            dma((2, nrow - 1)),
            dma((2, nrow - 1)),
            dma((2, group - 1)),
            dma((2, group - 1)),
            dma((2, nrow - 1)),
        ],
        compiler_params=pltpu.CompilerParams(
            collective_id=0, has_side_effects=True, vmem_limit_bytes=VMEM_BUDGET
        ),
    )(block_counts, block_coords[0, 0].T, features.T, weight, cotangent, blocks)
    activations, input_grad_t, weight_grad = pl.pallas_call(
        keep_kernel,
        out_shape=tuple(jax.ShapeDtypeStruct(x.shape, x.dtype) for x in outs),
        in_specs=[vmem()] * 3,
        out_specs=(vmem(),) * 3,
    )(*outs)
    return activations, input_grad_t.T, weight_grad


def fits(mesh, features, weight, cotangent, block_values):
    nrow, ncol, nrep = (mesh.shape[name] for name in ("row", "col", "rep"))
    group = ncol * nrep
    width = features.shape[1]
    fw = width // nrow
    rows, cols = cotangent.shape[0] // nrow, features.shape[0] // group
    tile = rows * cols * 2 + block_values.shape[2] * 128 * 128 * 6
    moved = 8 * rows * width + 12 * cols * width
    whole = nrep % 2 == 0 and block_values.shape[2] == 128 and rows * cols % 128**3 == 0
    whole = whole and (width // nrow) % (8 * group) == 0
    return whole and nrow > 1 and group > 2 and tile + moved < VMEM_BUDGET * 3 // 4


def solution(mesh):
    in_specs = (
        P(("col", "rep"), "row"),
        P(),
        P(("row", "col", "rep"), None),
        P("row", ("col", "rep"), None, None, None),
        P("row", ("col", "rep"), None, None),
        P("row", ("col", "rep")),
    )
    out_specs = (P(("row", "col", "rep"), None), P(("col", "rep"), "row"), P())
    sizes = tuple(mesh.shape[name] for name in ("row", "col", "rep"))

    def run(features, weight, cotangent, block_values, block_coords, block_counts):
        if fits(mesh, features, weight, cotangent, block_values):
            body = functools.partial(local_kernel, sizes)
        else:
            body = local_xla
        return jax.shard_map(
            body, mesh=mesh, in_specs=in_specs, out_specs=out_specs, check_vma=False
        )(features, weight, cotangent, block_values, block_coords, block_counts)

    return run
```

```python
import functools
import math

import jax
import jax.numpy as jnp
from jax import lax
from jax.experimental import pallas as pl
from jax.experimental.pallas import tpu as pltpu
from jax.sharding import PartitionSpec as P


def local_xla(features, weight, cotangent, block_values, block_coords, block_counts):
    blocks = block_values[0, 0]
    coords = block_coords[0, 0]
    live_count = block_counts[0, 0]
    slots = blocks.shape[0]
    gathered = lax.all_gather(features, "row", axis=1, tiled=True)
    feat_width = gathered.shape[1]
    col_blocks = gathered.shape[0] // 128
    row_blocks = cotangent.shape[0] * lax.axis_size(("col", "rep")) // 128
    feat_blocks = gathered.reshape(col_blocks, 128, feat_width)
    is_live = (jnp.arange(slots, dtype=jnp.int32) < live_count).astype(jnp.float32)
    per_turn = math.gcd(slots, 64)
    rounds = slots // per_turn
    pieces = (
        blocks.reshape(rounds, per_turn, 128, 128),
        coords[:, 0].reshape(rounds, per_turn),
        coords[:, 1].reshape(rounds, per_turn),
        is_live.reshape(rounds, per_turn),
    )

    def forward_step(total, piece):
        blocks_g, rows_g, cols_g, live_g = piece
        chosen = feat_blocks[cols_g]
        product = jnp.einsum("bij,bjf->bif", blocks_g, chosen, preferred_element_type=jnp.float32)
        return (total.at[rows_g].add(product * live_g[:, None, None]), None)

    partial_value, _ = lax.scan(
        forward_step, jnp.zeros((row_blocks, 128, feat_width), jnp.float32), pieces
    )
    partial_value = partial_value.reshape(row_blocks * 128, feat_width)
    summed = lax.psum_scatter(partial_value, ("col", "rep"), scatter_dimension=0, tiled=True)
    aggregate = summed.astype(jnp.bfloat16)
    pre_act = jnp.dot(aggregate, weight, preferred_element_type=jnp.float32)
    sigma = jax.nn.sigmoid(pre_act)
    activations = (pre_act * sigma).astype(jnp.bfloat16)
    grad_pre = (cotangent.astype(jnp.float32) * sigma * (1.0 + pre_act * (1.0 - sigma))).astype(
        jnp.bfloat16
    )
    weight_terms = jnp.dot(aggregate.T, grad_pre, preferred_element_type=jnp.float32)
    share = lax.psum_scatter(
        weight_terms.astype(jnp.bfloat16), ("col", "rep"), scatter_dimension=0, tiled=True
    ).astype(jnp.float32)
    share = lax.psum(share, "row")
    weight_grad = lax.all_gather(share, ("col", "rep"), axis=0, tiled=True)
    back_rows = jnp.dot(grad_pre, weight.T, preferred_element_type=jnp.float32).astype(jnp.bfloat16)
    back_all = lax.all_gather(back_rows, ("col", "rep"), axis=0, tiled=True)
    back_blocks = back_all.reshape(row_blocks, 128, back_all.shape[1])

    def backward_step(total, piece):
        blocks_g, rows_g, cols_g, live_g = piece
        chosen = back_blocks[rows_g]
        product = jnp.einsum("bji,bjf->bif", blocks_g, chosen, preferred_element_type=jnp.float32)
        return (total.at[cols_g].add(product * live_g[:, None, None]), None)

    grad_terms, _ = lax.scan(
        backward_step, jnp.zeros((col_blocks, 128, back_all.shape[1]), jnp.float32), pieces
    )
    grad_terms = grad_terms.reshape(col_blocks * 128, back_all.shape[1])
    input_grad = lax.psum_scatter(
        grad_terms.astype(jnp.bfloat16), "row", scatter_dimension=1, tiled=True
    )
    return (activations, input_grad, weight_grad)


BF16 = jnp.bfloat16
F32 = jnp.float32
VMEM_BUDGET = 60 * 2**20
MESH = pl.DeviceIdType.MESH


def dot(a, b, ca=1, cb=0):
    return lax.dot_general(a, b, (((ca,), (cb,)), ((), ())), preferred_element_type=F32)


def layer_kernel(
    sizes,
    count_in,
    coords_in,
    feat_in,
    weight_in,
    cot_in,
    blocks_hbm,
    act_out,
    igrad_out,
    wgrad_out,
    fbuf,
    bbuf,
    sums,
    dense,
    feat,
    pbuf,
    prec,
    qbuf,
    qrec,
    own_back,
    brec,
    bpar,
    total,
    zbuf,
    zrec,
    wbuf,
    wrec,
    shard_buf,
    srec,
    wall,
    tvec,
    table,
    load_sem,
    t_sem,
    f_sem,
    p_sem,
    q_sem,
    b_sem,
    c_sem,
    z_sem,
    w_sem,
    s_sem,
    g_sem,
):
    nrow, ncol, nrep = sizes
    nh = nrep // 2
    group = ncol * nrep
    slots = bbuf.shape[0]
    nodes, width = act_out.shape
    fw, col_nodes = feat_in.shape
    row_blocks, col_blocks = dense.shape[0] // 128, dense.shape[1] // 128
    r, c, p = lax.axis_index("row"), lax.axis_index("col"), lax.axis_index("rep")
    h, k = p // 2, p % 2
    g = c * nrep + p
    partner = h * 2 + (1 - k)
    offsets = [(dc, dh) for dc in reversed(range(ncol)) for dh in reversed(range(nh))]
    chips = len(offsets)

    def to_row(j):
        return {"row": (r + j) % nrow}

    def to_group(j):
        q = (g + j) % group
        return {"col": q // nrep, "rep": q % nrep}

    def to_chip(i):
        dc, dh = offsets[i]
        return {"col": (c + dc) % ncol, "rep": ((h + dh) % nh) * 2 + k}

    def part_to(i, core):
        dc, dh = offsets[i]
        return ((c + dc) % ncol) * nrep + ((h + dh) % nh) * 2 + core

    def part_from(i, core):
        dc, dh = offsets[i]
        return ((c + ncol - dc) % ncol) * nrep + ((h + nh - dh) % nh) * 2 + core

    def nearest(n):
        code = 0
        for q in range(nrow):
            order = sorted(range(nrow), key=lambda t: (abs(t - q), t))
            code += order[n] * nrow**q
        power = 1
        for q in range(1, nrow):
            power = power * jnp.where(r >= q, nrow, 1)
        return (code // power) % nrow

    def rcopy(src, dst, sems, i, device):
        return pltpu.make_async_remote_copy(
            src_ref=src,
            dst_ref=dst,
            send_sem=sems.at[0, i],
            recv_sem=sems.at[1, i],
            device_id=device,
            device_id_type=MESH,
        )

    chunks = load_sem.shape[0]
    per = slots // chunks
    loads = []
    for i in range(chunks):
        span = pl.ds(i * per, per)
        loads.append(pltpu.make_async_copy(blocks_hbm.at[span], bbuf.at[span], load_sem.at[i]))
        loads[-1].start()

    barrier = pltpu.get_barrier_semaphore()
    for j in range(1, nrow):
        pl.semaphore_signal(barrier, inc=1, device_id=to_row(j), device_id_type=MESH)
    for j in range(1, group):
        pl.semaphore_signal(barrier, inc=1, device_id=to_group(j), device_id_type=MESH)

    pl.semaphore_wait(barrier, nrow - 1 + group - 1)
    fcopies = []
    for side in range(2):
        there = r > 0 if side == 0 else r < nrow - 1
        copy = rcopy(feat_in, fbuf.at[r], f_sem.at[side], r, {"row": (r + nrow - 1 + 2 * side) % nrow})
        fcopies.append((there, copy))

        @pl.when(there)
        def _(copy=copy):
            copy.start()

    fbuf[r] = feat_in[...]

    places = row_blocks * col_blocks
    live = count_in[0, 0]
    row_form = coords_in[0:1, :] * col_blocks + coords_in[1:2, :]
    column_form = jnp.broadcast_to(row_form, (slots, slots)).T
    mine_at = lax.broadcasted_iota(jnp.int32, (slots, slots), 0)
    other_at = lax.broadcasted_iota(jnp.int32, (slots, slots), 1)
    hit = (column_form == row_form) & (mine_at < jnp.minimum(other_at, live))
    tvec[0:1, 0:slots] = jnp.max(jnp.where(hit, mine_at + 1, 0), axis=0, keepdims=True)
    for start in range(0, places, slots):
        hit = (column_form == other_at + start) & (mine_at < live)
        tvec[0:1, slots + start : 2 * slots + start] = jnp.max(
            jnp.where(hit, mine_at + 1, 0), axis=0, keepdims=True
        )
    tcopy = pltpu.make_async_copy(tvec, table, t_sem)
    tcopy.start()
    tcopy.wait()

    sums[0] = jnp.zeros((128, 128), F32)
    for i in range(chunks):
        loads[i].wait()

        def add_slot(s, carry):
            sums[s + 1] = sums[table[0, s]] + bbuf[s].astype(F32)
            return carry

        lax.fori_loop(i * per, (i + 1) * per, add_slot, 0)

    def fill(rb, carry):
        for cb in range(col_blocks):
            block = sums[table[0, slots + rb * col_blocks + cb]]
            dense[pl.ds(rb * 128, 128), cb * 128 : (cb + 1) * 128] = block.astype(BF16)
        return carry

    lax.fori_loop(0, row_blocks, fill, 0)

    half = nodes // 2

    def partial(part, slot):
        x = dot(dense[pl.ds(part * nodes, nodes), :], fbuf[slot], 1, 1)
        return jnp.concatenate([x[:half], x[half:]], axis=1)

    qcopies = []

    def merge(n, pcopy, mine):
        pcopy.wait()
        for i in range(chips - 1):
            qbuf[n, i] = (mine[i] + prec[n, i].astype(F32)).astype(BF16)
            copy = rcopy(qbuf.at[n, i], qrec.at[n, i], q_sem.at[n], i, to_chip(i))
            copy.start()
            qcopies.append(copy)
        return mine[chips - 1] + prec[n, chips - 1].astype(F32)

    held, waiting = [], None
    for n in range(nrow):
        slot = nearest(n)
        if n > 0:
            side = (slot < r).astype(jnp.int32)
            there = jnp.where(slot < r, r < nrow - 1, r > 0)
            copy = rcopy(
                fbuf.at[slot], fbuf.at[slot], f_sem.at[side], slot, {"row": (r + nrow - 1 + 2 * side) % nrow}
            )
            copy.wait_recv()
            fcopies.append((there, copy))

            @pl.when(there)
            def _(copy=copy):
                copy.start()

        for i in range(chips):
            pbuf[n, i] = partial(part_to(i, 1 - k), slot).astype(BF16)
        pcopy = rcopy(pbuf.at[n], prec.at[n], p_sem, n, {"rep": partner})
        pcopy.start()
        if waiting is not None:
            held.append(merge(*waiting))
        waiting = (n, pcopy, [partial(part_to(i, k), slot) for i in range(chips)])
    held.append(merge(*waiting))
    for there, copy in fcopies:

        @pl.when(there)
        def _(copy=copy):
            copy.wait_send()

    for n in range(nrow):
        got = held[n]
        for i in range(chips - 1):
            qcopies[n * (chips - 1) + i].wait()
            got = got + qrec[n, i].astype(F32)
        feat[nearest(n)] = got.astype(BF16)

    spread = jnp.concatenate([feat[m] for m in range(nrow)], axis=1)
    pieces = [spread[:, m * fw : (m + 1) * fw] for m in range(2 * nrow)]
    aggregate = jnp.concatenate(
        [jnp.concatenate(pieces[0::2], axis=1), jnp.concatenate(pieces[1::2], axis=1)], axis=0
    )
    pre_act = dot(aggregate, weight_in[...])
    sigma = jax.nn.sigmoid(pre_act)
    grad_pre = (cot_in[...].astype(F32) * sigma * (1.0 + pre_act * (1.0 - sigma))).astype(BF16)
    own_back[...] = dot(weight_in[...], grad_pre, 1, 1).astype(BF16)
    bcopies, ccopies = [], []
    for i in range(chips - 1):
        bcopies.append(rcopy(own_back, brec.at[i], b_sem, i, to_chip(i)))
        bcopies[i].start()
    first = rcopy(own_back, bpar.at[chips - 1], c_sem, chips - 1, {"rep": partner})
    first.start()

    terms = dot(aggregate, grad_pre, 0, 0)
    srows = width // group
    wbuf[...] = terms.astype(BF16).reshape(group, srows, width)
    wcopies = []
    for j in range(1, group):
        wcopies.append(rcopy(wbuf.at[(g + j) % group], wrec.at[j - 1], w_sem, j - 1, to_group(j)))
        wcopies[-1].start()
    act_out[...] = (pre_act * sigma).astype(BF16)

    def back_term(piece_t, part):
        return dot(piece_t, dense[pl.ds(part * nodes, nodes), :])

    total[...] = back_term(own_back[...], g)
    first.wait()
    total[...] += back_term(bpar[chips - 1], c * nrep + partner)

    for i in reversed(range(chips - 1)):
        bcopies[i].wait()
        ccopies.append(rcopy(brec.at[i], bpar.at[i], c_sem, i, {"rep": partner}))
        ccopies[-1].start()
        total[...] += back_term(brec[i], part_from(i, k))

    share = wbuf[g].astype(F32)
    for j in range(group - 1):
        wcopies[j].wait()
        share = share + wrec[j].astype(F32)
    shard_buf[...] = share.astype(BF16)
    scopies = []
    for j in range(1, nrow):
        scopies.append(rcopy(shard_buf, srec.at[j - 1], s_sem, j - 1, to_row(j)))
        scopies[-1].start()

    for n, i in enumerate(reversed(range(chips - 1))):
        ccopies[n].wait()
        total[...] += back_term(bpar[i], part_from(i, 1 - k))

    zcopies = []
    for j in range(1, nrow):
        q = (r + j) % nrow
        zbuf[j - 1] = total[pl.ds(q * fw, fw), :].astype(BF16)
        zcopies.append(rcopy(zbuf.at[j - 1], zrec.at[j - 1], z_sem, j - 1, to_row(j)))
        zcopies[-1].start()

    for j in range(nrow - 1):
        scopies[j].wait()
        share = share + srec[j].astype(F32)
    wall[g] = share
    gcopies = []
    for j in range(1, group):
        gcopies.append(rcopy(wall.at[g], wall.at[g], g_sem, j - 1, to_group(j)))
        gcopies[-1].start()

    mine = total[pl.ds(r * fw, fw), :]
    for j in range(nrow - 1):
        zcopies[j].wait()
        mine = mine + zrec[j].astype(F32)
    igrad_out[...] = mine.astype(BF16)
    for copy in gcopies:
        copy.wait()
    wgrad_out[...] = wall[...].reshape(width, width)


def keep_kernel(a_in, b_in, c_in, a_out, b_out, c_out):
    a_out[...] = a_in[...]
    b_out[...] = b_in[...]
    c_out[...] = c_in[...]


def local_kernel(sizes, features, weight, cotangent, block_values, block_coords, block_counts):
    nrow, ncol, nrep = sizes
    group = ncol * nrep
    chips = group // 2
    blocks = block_values[0, 0]
    slots = blocks.shape[0]
    nodes, width = cotangent.shape
    col_nodes, fw = features.shape
    row_blocks = nodes * group // 128
    places = row_blocks * (col_nodes // 128)
    chunks = math.gcd(slots, 8)
    srows = width // group
    square = (nodes, width)
    half = (nodes // 2, 2 * fw)
    vmem = functools.partial(pl.BlockSpec, memory_space=pltpu.VMEM)
    dma = pltpu.SemaphoreType.DMA
    outs = pl.pallas_call(
        functools.partial(layer_kernel, sizes),
        out_shape=(
            jax.ShapeDtypeStruct(square, BF16),
            jax.ShapeDtypeStruct((fw, col_nodes), BF16),
            jax.ShapeDtypeStruct((width, width), F32),
        ),
        in_specs=[
            pl.BlockSpec(memory_space=pltpu.SMEM),
            vmem(),
            vmem(),
            vmem(),
            vmem(),
            pl.BlockSpec(memory_space=pl.ANY),
        ],
        out_specs=(vmem(), vmem(), vmem()),
        scratch_shapes=[
            pltpu.VMEM((nrow, fw, col_nodes), BF16),
            pltpu.VMEM((slots, 128, 128), BF16),
            pltpu.VMEM((slots + 1, 128, 128), F32),
            pltpu.VMEM((row_blocks * 128, col_nodes), BF16),
            pltpu.VMEM((nrow,) + half, BF16),
            pltpu.VMEM((nrow, chips) + half, BF16),
            pltpu.VMEM((nrow, chips) + half, BF16),
            pltpu.VMEM((nrow, chips - 1) + half, BF16),
            pltpu.VMEM((nrow, chips - 1) + half, BF16),
            pltpu.VMEM((width, nodes), BF16),
            pltpu.VMEM((chips - 1, width, nodes), BF16),
            pltpu.VMEM((chips, width, nodes), BF16),
            pltpu.VMEM((width, col_nodes), F32),
            pltpu.VMEM((nrow - 1, fw, col_nodes), BF16),
            pltpu.VMEM((nrow - 1, fw, col_nodes), BF16),
            pltpu.VMEM((group, srows, width), BF16),
            pltpu.VMEM((group - 1, srows, width), BF16),
            pltpu.VMEM((srows, width), BF16),
            pltpu.VMEM((nrow - 1, srows, width), BF16),
            pltpu.VMEM((group, srows, width), F32),
            pltpu.VMEM((1, slots + places), jnp.int32),
            pltpu.SMEM((1, slots + places), jnp.int32),
            dma((chunks,)),
            dma,
            dma((2, 2, nrow)),
            dma((2, nrow)),
            dma((nrow, 2, chips - 1)),
            dma((2, chips - 1)),
            dma((2, chips)),
            dma((2, nrow - 1)),
            dma((2, group - 1)),
            dma((2, nrow - 1)),
            dma((2, group - 1)),
        ],
        compiler_params=pltpu.CompilerParams(
            collective_id=0, has_side_effects=True, vmem_limit_bytes=VMEM_BUDGET
        ),
    )(block_counts, block_coords[0, 0].T, features.T, weight, cotangent, blocks)
    activations, input_grad_t, weight_grad = pl.pallas_call(
        keep_kernel,
        out_shape=tuple(jax.ShapeDtypeStruct(x.shape, x.dtype) for x in outs),
        in_specs=[vmem()] * 3,
        out_specs=(vmem(),) * 3,
    )(*outs)
    return activations, input_grad_t.T, weight_grad


def fits(mesh, features, weight, cotangent, block_values):
    nrow, ncol, nrep = (mesh.shape[name] for name in ("row", "col", "rep"))
    group = ncol * nrep
    width = features.shape[1]
    fw = width // nrow
    rows, cols = cotangent.shape[0] // nrow, features.shape[0] // group
    tile = rows * cols * 2 + block_values.shape[2] * 128 * 128 * 6
    moved = 8 * rows * width + 12 * cols * width
    whole = nrep % 2 == 0 and block_values.shape[2] == 128 and rows * cols % 128**3 == 0
    whole = whole and 2 * fw == 128 and width % (16 * group) == 0
    return whole and nrow > 1 and group > 2 and tile + moved < VMEM_BUDGET * 3 // 4


def solution(mesh):
    in_specs = (
        P(("col", "rep"), "row"),
        P(),
        P(("row", "col", "rep"), None),
        P("row", ("col", "rep"), None, None, None),
        P("row", ("col", "rep"), None, None),
        P("row", ("col", "rep")),
    )
    out_specs = (P(("row", "col", "rep"), None), P(("col", "rep"), "row"), P())
    sizes = tuple(mesh.shape[name] for name in ("row", "col", "rep"))

    def run(features, weight, cotangent, block_values, block_coords, block_counts):
        if fits(mesh, features, weight, cotangent, block_values):
            body = functools.partial(local_kernel, sizes)
        else:
            body = local_xla
        return jax.shard_map(
            body, mesh=mesh, in_specs=in_specs, out_specs=out_specs, check_vma=False
        )(features, weight, cotangent, block_values, block_coords, block_counts)

    return run
```

```python
import functools
import math

import jax
import jax.numpy as jnp
from jax import lax
from jax.experimental import pallas as pl
from jax.experimental.pallas import tpu as pltpu
from jax.sharding import PartitionSpec as P


def local_xla(features, weight, cotangent, block_values, block_coords, block_counts):
    blocks = block_values[0, 0]
    coords = block_coords[0, 0]
    live_count = block_counts[0, 0]
    slots = blocks.shape[0]
    gathered = lax.all_gather(features, "row", axis=1, tiled=True)
    feat_width = gathered.shape[1]
    col_blocks = gathered.shape[0] // 128
    row_blocks = cotangent.shape[0] * lax.axis_size(("col", "rep")) // 128
    feat_blocks = gathered.reshape(col_blocks, 128, feat_width)
    is_live = (jnp.arange(slots, dtype=jnp.int32) < live_count).astype(jnp.float32)
    per_turn = math.gcd(slots, 64)
    rounds = slots // per_turn
    pieces = (
        blocks.reshape(rounds, per_turn, 128, 128),
        coords[:, 0].reshape(rounds, per_turn),
        coords[:, 1].reshape(rounds, per_turn),
        is_live.reshape(rounds, per_turn),
    )

    def forward_step(total, piece):
        blocks_g, rows_g, cols_g, live_g = piece
        chosen = feat_blocks[cols_g]
        product = jnp.einsum("bij,bjf->bif", blocks_g, chosen, preferred_element_type=jnp.float32)
        return (total.at[rows_g].add(product * live_g[:, None, None]), None)

    partial_value, _ = lax.scan(
        forward_step, jnp.zeros((row_blocks, 128, feat_width), jnp.float32), pieces
    )
    partial_value = partial_value.reshape(row_blocks * 128, feat_width)
    summed = lax.psum_scatter(partial_value, ("col", "rep"), scatter_dimension=0, tiled=True)
    aggregate = summed.astype(jnp.bfloat16)
    pre_act = jnp.dot(aggregate, weight, preferred_element_type=jnp.float32)
    sigma = jax.nn.sigmoid(pre_act)
    activations = (pre_act * sigma).astype(jnp.bfloat16)
    grad_pre = (cotangent.astype(jnp.float32) * sigma * (1.0 + pre_act * (1.0 - sigma))).astype(
        jnp.bfloat16
    )
    weight_terms = jnp.dot(aggregate.T, grad_pre, preferred_element_type=jnp.float32)
    share = lax.psum_scatter(
        weight_terms.astype(jnp.bfloat16), ("col", "rep"), scatter_dimension=0, tiled=True
    ).astype(jnp.float32)
    share = lax.psum(share, "row")
    weight_grad = lax.all_gather(share, ("col", "rep"), axis=0, tiled=True)
    back_rows = jnp.dot(grad_pre, weight.T, preferred_element_type=jnp.float32).astype(jnp.bfloat16)
    back_all = lax.all_gather(back_rows, ("col", "rep"), axis=0, tiled=True)
    back_blocks = back_all.reshape(row_blocks, 128, back_all.shape[1])

    def backward_step(total, piece):
        blocks_g, rows_g, cols_g, live_g = piece
        chosen = back_blocks[rows_g]
        product = jnp.einsum("bji,bjf->bif", blocks_g, chosen, preferred_element_type=jnp.float32)
        return (total.at[cols_g].add(product * live_g[:, None, None]), None)

    grad_terms, _ = lax.scan(
        backward_step, jnp.zeros((col_blocks, 128, back_all.shape[1]), jnp.float32), pieces
    )
    grad_terms = grad_terms.reshape(col_blocks * 128, back_all.shape[1])
    input_grad = lax.psum_scatter(
        grad_terms.astype(jnp.bfloat16), "row", scatter_dimension=1, tiled=True
    )
    return (activations, input_grad, weight_grad)


BF16 = jnp.bfloat16
F32 = jnp.float32
VMEM_BUDGET = 60 * 2**20
MESH = pl.DeviceIdType.MESH


def dot(a, b, ca=1, cb=0):
    return lax.dot_general(a, b, (((ca,), (cb,)), ((), ())), preferred_element_type=F32)


def layer_kernel(
    sizes,
    count_in,
    coords_in,
    feat_in,
    weight_in,
    cot_in,
    blocks_hbm,
    act_out,
    igrad_out,
    wgrad_out,
    fbuf,
    bbuf,
    sums,
    dense,
    feat,
    pbuf,
    prec,
    qbuf,
    qrec,
    own_back,
    brec,
    bpar,
    total,
    zbuf,
    zrec,
    wbuf,
    wrec,
    shard_buf,
    srec,
    wall,
    tvec,
    table,
    load_sem,
    t_sem,
    f_sem,
    p_sem,
    q_sem,
    b_sem,
    c_sem,
    z_sem,
    w_sem,
    s_sem,
    g_sem,
):
    nrow, ncol, nrep = sizes
    nh = nrep // 2
    group = ncol * nrep
    slots = bbuf.shape[0]
    nodes, width = act_out.shape
    fw, col_nodes = feat_in.shape
    row_blocks, col_blocks = dense.shape[0] // 128, dense.shape[1] // 128
    r, c, p = lax.axis_index("row"), lax.axis_index("col"), lax.axis_index("rep")
    h, k = p // 2, p % 2
    g = c * nrep + p
    partner = h * 2 + (1 - k)
    offsets = [(dc, dh) for dc in reversed(range(ncol)) for dh in reversed(range(nh))]
    chips = len(offsets)

    def to_row(j):
        return {"row": (r + j) % nrow}

    def to_group(j):
        q = (g + j) % group
        return {"col": q // nrep, "rep": q % nrep}

    def to_chip(i):
        dc, dh = offsets[i]
        return {"col": (c + dc) % ncol, "rep": ((h + dh) % nh) * 2 + k}

    def part_to(i, core):
        dc, dh = offsets[i]
        return ((c + dc) % ncol) * nrep + ((h + dh) % nh) * 2 + core

    def part_from(i, core):
        dc, dh = offsets[i]
        return ((c + ncol - dc) % ncol) * nrep + ((h + nh - dh) % nh) * 2 + core

    def nearest(n):
        code = 0
        for q in range(nrow):
            order = sorted(range(nrow), key=lambda t: (abs(t - q), t))
            code += order[n] * nrow**q
        power = 1
        for q in range(1, nrow):
            power = power * jnp.where(r >= q, nrow, 1)
        return (code // power) % nrow

    def rcopy(src, dst, sems, i, device):
        return pltpu.make_async_remote_copy(
            src_ref=src,
            dst_ref=dst,
            send_sem=sems.at[0, i],
            recv_sem=sems.at[1, i],
            device_id=device,
            device_id_type=MESH,
        )

    chunks = load_sem.shape[0]
    per = slots // chunks
    loads = []
    for i in range(chunks):
        span = pl.ds(i * per, per)
        loads.append(pltpu.make_async_copy(blocks_hbm.at[span], bbuf.at[span], load_sem.at[i]))
        loads[-1].start()

    barrier = pltpu.get_barrier_semaphore()
    for j in range(1, nrow):
        pl.semaphore_signal(barrier, inc=1, device_id=to_row(j), device_id_type=MESH)
    for j in range(1, group):
        pl.semaphore_signal(barrier, inc=1, device_id=to_group(j), device_id_type=MESH)

    pl.semaphore_wait(barrier, nrow - 1 + group - 1)
    fcopies = []
    for side in range(2):
        there = r > 0 if side == 0 else r < nrow - 1
        copy = rcopy(feat_in, fbuf.at[r], f_sem.at[side], r, {"row": (r + nrow - 1 + 2 * side) % nrow})
        fcopies.append((there, copy))

        @pl.when(there)
        def _(copy=copy):
            copy.start()

    fbuf[r] = feat_in[...]

    places = row_blocks * col_blocks
    live = count_in[0, 0]
    row_form = coords_in[0:1, :] * col_blocks + coords_in[1:2, :]
    column_form = jnp.broadcast_to(row_form, (slots, slots)).T
    mine_at = lax.broadcasted_iota(jnp.int32, (slots, slots), 0)
    other_at = lax.broadcasted_iota(jnp.int32, (slots, slots), 1)
    hit = (column_form == row_form) & (mine_at < jnp.minimum(other_at, live))
    tvec[0:1, 0:slots] = jnp.max(jnp.where(hit, mine_at + 1, 0), axis=0, keepdims=True)
    for start in range(0, places, slots):
        hit = (column_form == other_at + start) & (mine_at < live)
        tvec[0:1, slots + start : 2 * slots + start] = jnp.max(
            jnp.where(hit, mine_at + 1, 0), axis=0, keepdims=True
        )
    tcopy = pltpu.make_async_copy(tvec, table, t_sem)
    tcopy.start()
    tcopy.wait()

    sums[0] = jnp.zeros((128, 128), F32)
    for i in range(chunks):
        loads[i].wait()

        def add_slot(s, carry):
            sums[s + 1] = sums[table[0, s]] + bbuf[s].astype(F32)
            return carry

        lax.fori_loop(i * per, (i + 1) * per, add_slot, 0)

    def fill(rb, carry):
        for cb in range(col_blocks):
            block = sums[table[0, slots + rb * col_blocks + cb]]
            dense[pl.ds(rb * 128, 128), cb * 128 : (cb + 1) * 128] = block.astype(BF16)
        return carry

    lax.fori_loop(0, row_blocks, fill, 0)

    half = nodes // 2

    def partial(part, slot):
        x = dot(dense[pl.ds(part * nodes, nodes), :], fbuf[slot], 1, 1)
        return jnp.concatenate([x[:half], x[half:]], axis=1)

    qcopies = []

    def merge(n, pcopy, mine):
        pcopy.wait()
        for i in range(chips - 1):
            qbuf[n, i] = (mine[i] + prec[n, i].astype(F32)).astype(BF16)
            copy = rcopy(qbuf.at[n, i], qrec.at[n, i], q_sem.at[n], i, to_chip(i))
            copy.start()
            qcopies.append(copy)
        return mine[chips - 1] + prec[n, chips - 1].astype(F32)

    held, waiting = [], None
    for n in range(nrow):
        slot = nearest(n)
        if n > 0:
            side = (slot < r).astype(jnp.int32)
            there = jnp.where(slot < r, r < nrow - 1, r > 0)
            copy = rcopy(
                fbuf.at[slot], fbuf.at[slot], f_sem.at[side], slot, {"row": (r + nrow - 1 + 2 * side) % nrow}
            )
            copy.wait_recv()
            fcopies.append((there, copy))

            @pl.when(there)
            def _(copy=copy):
                copy.start()

        for i in range(chips):
            pbuf[n, i] = partial(part_to(i, 1 - k), slot).astype(BF16)
        pcopy = rcopy(pbuf.at[n], prec.at[n], p_sem, n, {"rep": partner})
        pcopy.start()
        if waiting is not None:
            held.append(merge(*waiting))
        waiting = (n, pcopy, [partial(part_to(i, k), slot) for i in range(chips)])
    held.append(merge(*waiting))
    for there, copy in fcopies:

        @pl.when(there)
        def _(copy=copy):
            copy.wait_send()

    for n in range(nrow):
        got = held[n]
        for i in range(chips - 1):
            qcopies[n * (chips - 1) + i].wait()
            got = got + qrec[n, i].astype(F32)
        feat[nearest(n)] = got.astype(BF16)

    spread = jnp.concatenate([feat[m] for m in range(nrow)], axis=1)
    pieces = [spread[:, m * fw : (m + 1) * fw] for m in range(2 * nrow)]
    aggregate = jnp.concatenate(
        [jnp.concatenate(pieces[0::2], axis=1), jnp.concatenate(pieces[1::2], axis=1)], axis=0
    )
    pre_act = dot(aggregate, weight_in[...])
    sigma = jax.nn.sigmoid(pre_act)
    grad_pre = (cot_in[...].astype(F32) * sigma * (1.0 + pre_act * (1.0 - sigma))).astype(BF16)
    own_back[...] = dot(weight_in[...], grad_pre, 1, 1).astype(BF16).reshape(nrow, fw, nodes)
    bcopies, ccopies, firsts = [], [], []
    for m in range(nrow):
        q = nearest(nrow - 1 - m)
        bcopies.append([])
        for i in range(chips - 1):
            bcopies[m].append(rcopy(own_back.at[q], brec.at[m, i], b_sem.at[m], i, to_chip(i)))
            bcopies[m][i].start()
        firsts.append(
            rcopy(own_back.at[q], bpar.at[m, chips - 1], c_sem.at[m], chips - 1, {"rep": partner})
        )
        firsts[m].start()

    terms = dot(aggregate, grad_pre, 0, 0)
    srows = width // group
    wbuf[...] = terms.astype(BF16).reshape(group, srows, width)
    wcopies = []
    for j in range(1, group):
        wcopies.append(rcopy(wbuf.at[(g + j) % group], wrec.at[j - 1], w_sem, j - 1, to_group(j)))
        wcopies[-1].start()
    act_out[...] = (pre_act * sigma).astype(BF16)

    def back_term(piece_t, part):
        return dot(piece_t, dense[pl.ds(part * nodes, nodes), :])

    def pass_on(m):
        ccopies.append([])
        for i in reversed(range(chips - 1)):
            bcopies[m][i].wait()
            copy = rcopy(brec.at[m, i], bpar.at[m, i], c_sem.at[m], i, {"rep": partner})
            copy.start()
            ccopies[m].append(copy)

    def compute(m):
        own = back_term(own_back[nearest(nrow - 1 - m)], g)
        for i in reversed(range(chips - 1)):
            own = own + back_term(brec[m, i], part_from(i, k))
        firsts[m].wait()
        own = own + back_term(bpar[m, chips - 1], c * nrep + partner)
        for n, i in enumerate(reversed(range(chips - 1))):
            ccopies[m][n].wait()
            own = own + back_term(bpar[m, i], part_from(i, 1 - k))
        total[m] = own

    zparts = zbuf.shape[1]
    zcols = col_nodes // zparts
    zcopies = []

    def chain(m, later):
        q = nearest(nrow - 1 - m)
        side = (q > r).astype(jnp.int32)
        joined = jnp.where(q > r, r > 0, r < nrow - 1)
        target = {"row": (r + nrow - 1 + 2 * side) % nrow}

        @pl.when(joined if later else jnp.logical_not(joined))
        def _():
            for e in range(zparts):
                copy = rcopy(zbuf.at[q, e], zrec.at[side, q, e], z_sem.at[side, e], q, target)
                mine = total[m, :, e * zcols : (e + 1) * zcols]
                if later:
                    copy.wait_recv()
                    mine = mine + zrec[side, q, e].astype(F32)
                zbuf[q, e] = mine.astype(BF16)
                copy.start()

        if later:
            for e in range(zparts):
                zcopies.append(rcopy(zbuf.at[q, e], zrec.at[side, q, e], z_sem.at[side, e], q, target))

    for m in range(nrow):
        if m < 2:
            pass_on(m)
        if 1 <= m < nrow - 1:
            pass_on(m + 1)
        compute(m)
        if m < nrow - 1:
            chain(m, False)
        if m > 0:
            chain(m - 1, True)
        if m == 1:
            share = wbuf[g].astype(F32)
            for j in range(group - 1):
                wcopies[j].wait()
                share = share + wrec[j].astype(F32)
            shard_buf[...] = share.astype(BF16)
            scopies = []
            for j in range(1, nrow):
                scopies.append(rcopy(shard_buf, srec.at[j - 1], s_sem, j - 1, to_row(j)))
                scopies[-1].start()

    for j in range(nrow - 1):
        scopies[j].wait()
        share = share + srec[j].astype(F32)
    wall[g] = share
    gcopies = []
    for j in range(1, group):
        gcopies.append(rcopy(wall.at[g], wall.at[g], g_sem, j - 1, to_group(j)))
        gcopies[-1].start()

    for side in range(2):

        @pl.when(r > 0 if side == 1 else r < nrow - 1)
        def _(side=side):
            for e in range(zparts):
                came = rcopy(
                    zbuf.at[r, e], zrec.at[side, r, e], z_sem.at[side, e], r, {"row": (r + 1) % nrow}
                )
                came.wait_recv()
                cols = slice(e * zcols, (e + 1) * zcols)
                total[nrow - 1, :, cols] = total[nrow - 1, :, cols] + zrec[side, r, e].astype(F32)

    igrad_out[...] = total[nrow - 1].astype(BF16)
    for copy in zcopies:
        copy.wait_send()
    for copy in gcopies:
        copy.wait()
    wgrad_out[...] = wall[...].reshape(width, width)


def keep_kernel(a_in, b_in, c_in, a_out, b_out, c_out):
    a_out[...] = a_in[...]
    b_out[...] = b_in[...]
    c_out[...] = c_in[...]


def local_kernel(sizes, features, weight, cotangent, block_values, block_coords, block_counts):
    nrow, ncol, nrep = sizes
    group = ncol * nrep
    chips = group // 2
    blocks = block_values[0, 0]
    slots = blocks.shape[0]
    nodes, width = cotangent.shape
    col_nodes, fw = features.shape
    row_blocks = nodes * group // 128
    places = row_blocks * (col_nodes // 128)
    chunks = math.gcd(slots, 8)
    srows = width // group
    square = (nodes, width)
    zparts = 2
    half = (nodes // 2, 2 * fw)
    vmem = functools.partial(pl.BlockSpec, memory_space=pltpu.VMEM)
    dma = pltpu.SemaphoreType.DMA
    outs = pl.pallas_call(
        functools.partial(layer_kernel, sizes),
        out_shape=(
            jax.ShapeDtypeStruct(square, BF16),
            jax.ShapeDtypeStruct((fw, col_nodes), BF16),
            jax.ShapeDtypeStruct((width, width), F32),
        ),
        in_specs=[
            pl.BlockSpec(memory_space=pltpu.SMEM),
            vmem(),
            vmem(),
            vmem(),
            vmem(),
            pl.BlockSpec(memory_space=pl.ANY),
        ],
        out_specs=(vmem(), vmem(), vmem()),
        scratch_shapes=[
            pltpu.VMEM((nrow, fw, col_nodes), BF16),
            pltpu.VMEM((slots, 128, 128), BF16),
            pltpu.VMEM((slots + 1, 128, 128), F32),
            pltpu.VMEM((row_blocks * 128, col_nodes), BF16),
            pltpu.VMEM((nrow,) + half, BF16),
            pltpu.VMEM((nrow, chips) + half, BF16),
            pltpu.VMEM((nrow, chips) + half, BF16),
            pltpu.VMEM((nrow, chips - 1) + half, BF16),
            pltpu.VMEM((nrow, chips - 1) + half, BF16),
            pltpu.VMEM((nrow, fw, nodes), BF16),
            pltpu.VMEM((nrow, chips - 1, fw, nodes), BF16),
            pltpu.VMEM((nrow, chips, fw, nodes), BF16),
            pltpu.VMEM((nrow, fw, col_nodes), F32),
            pltpu.VMEM((nrow, zparts, fw, col_nodes // zparts), BF16),
            pltpu.VMEM((2, nrow, zparts, fw, col_nodes // zparts), BF16),
            pltpu.VMEM((group, srows, width), BF16),
            pltpu.VMEM((group - 1, srows, width), BF16),
            pltpu.VMEM((srows, width), BF16),
            pltpu.VMEM((nrow - 1, srows, width), BF16),
            pltpu.VMEM((group, srows, width), F32),
            pltpu.VMEM((1, slots + places), jnp.int32),
            pltpu.SMEM((1, slots + places), jnp.int32),
            dma((chunks,)),
            dma,
            dma((2, 2, nrow)),
            dma((2, nrow)),
            dma((nrow, 2, chips - 1)),
            dma((nrow, 2, chips - 1)),
            dma((nrow, 2, chips)),
            dma((2, zparts, 2, nrow)),
            dma((2, group - 1)),
            dma((2, nrow - 1)),
            dma((2, group - 1)),
        ],
        compiler_params=pltpu.CompilerParams(
            collective_id=0, has_side_effects=True, vmem_limit_bytes=VMEM_BUDGET
        ),
    )(block_counts, block_coords[0, 0].T, features.T, weight, cotangent, blocks)
    activations, input_grad_t, weight_grad = pl.pallas_call(
        keep_kernel,
        out_shape=tuple(jax.ShapeDtypeStruct(x.shape, x.dtype) for x in outs),
        in_specs=[vmem()] * 3,
        out_specs=(vmem(),) * 3,
    )(*outs)
    return activations, input_grad_t.T, weight_grad


def fits(mesh, features, weight, cotangent, block_values):
    nrow, ncol, nrep = (mesh.shape[name] for name in ("row", "col", "rep"))
    group = ncol * nrep
    width = features.shape[1]
    fw = width // nrow
    rows, cols = cotangent.shape[0] // nrow, features.shape[0] // group
    tile = rows * cols * 2 + block_values.shape[2] * 128 * 128 * 6
    moved = 8 * rows * width + 12 * cols * width
    whole = nrep % 2 == 0 and block_values.shape[2] == 128 and rows * cols % 128**3 == 0
    whole = whole and 2 * fw == 128 and width % (16 * group) == 0
    return whole and nrow > 1 and group > 2 and tile + moved < VMEM_BUDGET * 3 // 4


def solution(mesh):
    in_specs = (
        P(("col", "rep"), "row"),
        P(),
        P(("row", "col", "rep"), None),
        P("row", ("col", "rep"), None, None, None),
        P("row", ("col", "rep"), None, None),
        P("row", ("col", "rep")),
    )
    out_specs = (P(("row", "col", "rep"), None), P(("col", "rep"), "row"), P())
    sizes = tuple(mesh.shape[name] for name in ("row", "col", "rep"))

    def run(features, weight, cotangent, block_values, block_coords, block_counts):
        if fits(mesh, features, weight, cotangent, block_values):
            body = functools.partial(local_kernel, sizes)
        else:
            body = local_xla
        return jax.shard_map(
            body, mesh=mesh, in_specs=in_specs, out_specs=out_specs, check_vma=False
        )(features, weight, cotangent, block_values, block_coords, block_counts)

    return run
```

```python
import functools
import math

import jax
import jax.numpy as jnp
from jax import lax
from jax.experimental import pallas as pl
from jax.experimental.pallas import tpu as pltpu
from jax.sharding import PartitionSpec as P


def local_xla(features, weight, cotangent, block_values, block_coords, block_counts):
    blocks = block_values[0, 0]
    coords = block_coords[0, 0]
    live_count = block_counts[0, 0]
    slots = blocks.shape[0]
    gathered = lax.all_gather(features, "row", axis=1, tiled=True)
    feat_width = gathered.shape[1]
    col_blocks = gathered.shape[0] // 128
    row_blocks = cotangent.shape[0] * lax.axis_size(("col", "rep")) // 128
    feat_blocks = gathered.reshape(col_blocks, 128, feat_width)
    is_live = (jnp.arange(slots, dtype=jnp.int32) < live_count).astype(jnp.float32)
    per_turn = math.gcd(slots, 64)
    rounds = slots // per_turn
    pieces = (
        blocks.reshape(rounds, per_turn, 128, 128),
        coords[:, 0].reshape(rounds, per_turn),
        coords[:, 1].reshape(rounds, per_turn),
        is_live.reshape(rounds, per_turn),
    )

    def forward_step(total, piece):
        blocks_g, rows_g, cols_g, live_g = piece
        chosen = feat_blocks[cols_g]
        product = jnp.einsum("bij,bjf->bif", blocks_g, chosen, preferred_element_type=jnp.float32)
        return (total.at[rows_g].add(product * live_g[:, None, None]), None)

    partial_value, _ = lax.scan(
        forward_step, jnp.zeros((row_blocks, 128, feat_width), jnp.float32), pieces
    )
    partial_value = partial_value.reshape(row_blocks * 128, feat_width)
    summed = lax.psum_scatter(partial_value, ("col", "rep"), scatter_dimension=0, tiled=True)
    aggregate = summed.astype(jnp.bfloat16)
    pre_act = jnp.dot(aggregate, weight, preferred_element_type=jnp.float32)
    sigma = jax.nn.sigmoid(pre_act)
    activations = (pre_act * sigma).astype(jnp.bfloat16)
    grad_pre = (cotangent.astype(jnp.float32) * sigma * (1.0 + pre_act * (1.0 - sigma))).astype(
        jnp.bfloat16
    )
    weight_terms = jnp.dot(aggregate.T, grad_pre, preferred_element_type=jnp.float32)
    share = lax.psum_scatter(
        weight_terms.astype(jnp.bfloat16), ("col", "rep"), scatter_dimension=0, tiled=True
    ).astype(jnp.float32)
    share = lax.psum(share, "row")
    weight_grad = lax.all_gather(share, ("col", "rep"), axis=0, tiled=True)
    back_rows = jnp.dot(grad_pre, weight.T, preferred_element_type=jnp.float32).astype(jnp.bfloat16)
    back_all = lax.all_gather(back_rows, ("col", "rep"), axis=0, tiled=True)
    back_blocks = back_all.reshape(row_blocks, 128, back_all.shape[1])

    def backward_step(total, piece):
        blocks_g, rows_g, cols_g, live_g = piece
        chosen = back_blocks[rows_g]
        product = jnp.einsum("bji,bjf->bif", blocks_g, chosen, preferred_element_type=jnp.float32)
        return (total.at[cols_g].add(product * live_g[:, None, None]), None)

    grad_terms, _ = lax.scan(
        backward_step, jnp.zeros((col_blocks, 128, back_all.shape[1]), jnp.float32), pieces
    )
    grad_terms = grad_terms.reshape(col_blocks * 128, back_all.shape[1])
    input_grad = lax.psum_scatter(
        grad_terms.astype(jnp.bfloat16), "row", scatter_dimension=1, tiled=True
    )
    return (activations, input_grad, weight_grad)


BF16 = jnp.bfloat16
F32 = jnp.float32
VMEM_BUDGET = 60 * 2**20
MESH = pl.DeviceIdType.MESH


def dot(a, b, ca=1, cb=0):
    return lax.dot_general(a, b, (((ca,), (cb,)), ((), ())), preferred_element_type=F32)


def layer_kernel(
    sizes,
    count_in,
    coords_in,
    feat_in,
    weight_in,
    cot_in,
    blocks_hbm,
    act_out,
    igrad_out,
    wgrad_out,
    fbuf,
    bbuf,
    sums,
    dense,
    feat,
    pbuf,
    prec,
    qbuf,
    qrec,
    own_back,
    brec,
    bpar,
    total,
    zbuf,
    zrec,
    wbuf,
    wrec,
    shard_buf,
    srec,
    wall,
    tvec,
    table,
    load_sem,
    t_sem,
    f_sem,
    p_sem,
    q_sem,
    b_sem,
    c_sem,
    z_sem,
    w_sem,
    s_sem,
    g_sem,
):
    nrow, ncol, nrep = sizes
    nh = nrep // 2
    group = ncol * nrep
    slots = bbuf.shape[0]
    nodes, width = act_out.shape
    fw, col_nodes = feat_in.shape
    row_blocks, col_blocks = dense.shape[0] // 128, dense.shape[1] // 128
    r, c, p = lax.axis_index("row"), lax.axis_index("col"), lax.axis_index("rep")
    h, k = p // 2, p % 2
    g = c * nrep + p
    partner = h * 2 + (1 - k)
    offsets = [(dc, dh) for dc in reversed(range(ncol)) for dh in reversed(range(nh))]
    chips = len(offsets)

    def to_row(j):
        return {"row": (r + j) % nrow}

    def to_group(j):
        q = (g + j) % group
        return {"col": q // nrep, "rep": q % nrep}

    def to_chip(i):
        dc, dh = offsets[i]
        return {"col": (c + dc) % ncol, "rep": ((h + dh) % nh) * 2 + k}

    def part_to(i, core):
        dc, dh = offsets[i]
        return ((c + dc) % ncol) * nrep + ((h + dh) % nh) * 2 + core

    def part_from(i, core):
        dc, dh = offsets[i]
        return ((c + ncol - dc) % ncol) * nrep + ((h + nh - dh) % nh) * 2 + core

    def nearest(n):
        code = 0
        for q in range(nrow):
            order = sorted(range(nrow), key=lambda t: (abs(t - q), t))
            code += order[n] * nrow**q
        power = 1
        for q in range(1, nrow):
            power = power * jnp.where(r >= q, nrow, 1)
        return (code // power) % nrow

    def rcopy(src, dst, sems, i, device):
        return pltpu.make_async_remote_copy(
            src_ref=src,
            dst_ref=dst,
            send_sem=sems.at[0, i],
            recv_sem=sems.at[1, i],
            device_id=device,
            device_id_type=MESH,
        )

    chunks = load_sem.shape[0]
    per = slots // chunks
    loads = []
    for i in range(chunks):
        span = pl.ds(i * per, per)
        loads.append(pltpu.make_async_copy(blocks_hbm.at[span], bbuf.at[span], load_sem.at[i]))
        loads[-1].start()

    barrier = pltpu.get_barrier_semaphore()
    for j in range(1, nrow):
        pl.semaphore_signal(barrier, inc=1, device_id=to_row(j), device_id_type=MESH)
    for j in range(1, group):
        pl.semaphore_signal(barrier, inc=1, device_id=to_group(j), device_id_type=MESH)

    pl.semaphore_wait(barrier, nrow - 1 + group - 1)
    fcopies = []
    for side in range(2):
        there = r > 0 if side == 0 else r < nrow - 1
        copy = rcopy(feat_in, fbuf.at[r], f_sem.at[side], r, {"row": (r + nrow - 1 + 2 * side) % nrow})
        fcopies.append((there, copy))

        @pl.when(there)
        def _(copy=copy):
            copy.start()

    fbuf[r] = feat_in[...]

    places = row_blocks * col_blocks
    live = count_in[0, 0]
    row_form = coords_in[0:1, :] * col_blocks + coords_in[1:2, :]
    column_form = jnp.broadcast_to(row_form, (slots, slots)).T
    mine_at = lax.broadcasted_iota(jnp.int32, (slots, slots), 0)
    other_at = lax.broadcasted_iota(jnp.int32, (slots, slots), 1)
    hit = (column_form == row_form) & (mine_at < jnp.minimum(other_at, live))
    tvec[0:1, 0:slots] = jnp.max(jnp.where(hit, mine_at + 1, 0), axis=0, keepdims=True)
    for start in range(0, places, slots):
        hit = (column_form == other_at + start) & (mine_at < live)
        tvec[0:1, slots + start : 2 * slots + start] = jnp.max(
            jnp.where(hit, mine_at + 1, 0), axis=0, keepdims=True
        )
    tcopy = pltpu.make_async_copy(tvec, table, t_sem)
    tcopy.start()
    tcopy.wait()

    sums[0] = jnp.zeros((128, 128), F32)
    for i in range(chunks):
        loads[i].wait()

        def add_slot(s, carry):
            sums[s + 1] = sums[table[0, s]] + bbuf[s].astype(F32)
            return carry

        lax.fori_loop(i * per, (i + 1) * per, add_slot, 0)

    def fill(rb, carry):
        for cb in range(col_blocks):
            block = sums[table[0, slots + rb * col_blocks + cb]]
            dense[pl.ds(rb * 128, 128), cb * 128 : (cb + 1) * 128] = block.astype(BF16)
        return carry

    lax.fori_loop(0, row_blocks, fill, 0)

    half = nodes // 2

    def partial(part, slot):
        x = dot(dense[pl.ds(part * nodes, nodes), :], fbuf[slot], 1, 1)
        return jnp.concatenate([x[:half], x[half:]], axis=1)

    qcopies = []

    def merge(n, pcopy, mine):
        pcopy.wait()
        for i in range(chips - 1):
            qbuf[n, i] = (mine[i] + prec[n, i].astype(F32)).astype(BF16)
            copy = rcopy(qbuf.at[n, i], qrec.at[n, i], q_sem.at[n], i, to_chip(i))
            copy.start()
            qcopies.append(copy)
        return mine[chips - 1] + prec[n, chips - 1].astype(F32)

    held, waiting = [], None
    for n in range(nrow):
        slot = nearest(n)
        if n > 0:
            side = (slot < r).astype(jnp.int32)
            there = jnp.where(slot < r, r < nrow - 1, r > 0)
            copy = rcopy(
                fbuf.at[slot], fbuf.at[slot], f_sem.at[side], slot, {"row": (r + nrow - 1 + 2 * side) % nrow}
            )
            copy.wait_recv()
            fcopies.append((there, copy))

            @pl.when(there)
            def _(copy=copy):
                copy.start()

        for i in range(chips):
            pbuf[n, i] = partial(part_to(i, 1 - k), slot).astype(BF16)
        pcopy = rcopy(pbuf.at[n], prec.at[n], p_sem, n, {"rep": partner})
        pcopy.start()
        if waiting is not None:
            held.append(merge(*waiting))
        waiting = (n, pcopy, [partial(part_to(i, k), slot) for i in range(chips)])
    held.append(merge(*waiting))
    for there, copy in fcopies:

        @pl.when(there)
        def _(copy=copy):
            copy.wait_send()

    for n in range(nrow):
        got = held[n]
        for i in range(chips - 1):
            qcopies[n * (chips - 1) + i].wait()
            got = got + qrec[n, i].astype(F32)
        feat[nearest(n)] = got.astype(BF16)

    spread = jnp.concatenate([feat[m] for m in range(nrow)], axis=1)
    pieces = [spread[:, m * fw : (m + 1) * fw] for m in range(2 * nrow)]
    aggregate = jnp.concatenate(
        [jnp.concatenate(pieces[0::2], axis=1), jnp.concatenate(pieces[1::2], axis=1)], axis=0
    )
    pre_act = dot(aggregate, weight_in[...])
    sigma = jax.nn.sigmoid(pre_act)
    grad_pre = (cot_in[...].astype(F32) * sigma * (1.0 + pre_act * (1.0 - sigma))).astype(BF16)
    own_back[...] = dot(weight_in[...], grad_pre, 1, 1).astype(BF16).reshape(nrow, fw, nodes)
    bcopies, ccopies, firsts = [], [], []
    for m in range(nrow):
        q = nearest(nrow - 1 - m)
        bcopies.append([])
        for i in range(chips - 1):
            bcopies[m].append(rcopy(own_back.at[q], brec.at[m, i], b_sem.at[m], i, to_chip(i)))
            bcopies[m][i].start()
        firsts.append(
            rcopy(own_back.at[q], bpar.at[m, chips - 1], c_sem.at[m], chips - 1, {"rep": partner})
        )
        firsts[m].start()
        if m == 0:
            terms = dot(aggregate, grad_pre, 0, 0)
            srows = width // group
            wbuf[...] = terms.astype(BF16).reshape(group, srows, width)
            wcopies = []
            for j in range(1, group):
                wcopies.append(rcopy(wbuf.at[(g + j) % group], wrec.at[j - 1], w_sem, j - 1, to_group(j)))
                wcopies[-1].start()

    act_out[...] = (pre_act * sigma).astype(BF16)

    def back_term(piece_t, part):
        return dot(piece_t, dense[pl.ds(part * nodes, nodes), :])

    def pass_on(m):
        ccopies.append([])
        for i in reversed(range(chips - 1)):
            bcopies[m][i].wait()
            copy = rcopy(brec.at[m, i], bpar.at[m, i], c_sem.at[m], i, {"rep": partner})
            copy.start()
            ccopies[m].append(copy)

    def compute(m):
        own = back_term(own_back[nearest(nrow - 1 - m)], g)
        for i in reversed(range(chips - 1)):
            own = own + back_term(brec[m, i], part_from(i, k))
        firsts[m].wait()
        own = own + back_term(bpar[m, chips - 1], c * nrep + partner)
        for n, i in enumerate(reversed(range(chips - 1))):
            ccopies[m][n].wait()
            own = own + back_term(bpar[m, i], part_from(i, 1 - k))
        total[m] = own

    zparts = zbuf.shape[1]
    zcols = col_nodes // zparts
    zcopies = []

    def chain(m, later):
        q = nearest(nrow - 1 - m)
        side = (q > r).astype(jnp.int32)
        joined = jnp.where(q > r, r > 0, r < nrow - 1)
        target = {"row": (r + nrow - 1 + 2 * side) % nrow}

        @pl.when(joined if later else jnp.logical_not(joined))
        def _():
            for e in range(zparts):
                copy = rcopy(zbuf.at[q, e], zrec.at[side, q, e], z_sem.at[side, e], q, target)
                mine = total[m, :, e * zcols : (e + 1) * zcols]
                if later:
                    copy.wait_recv()
                    mine = mine + zrec[side, q, e].astype(F32)
                zbuf[q, e] = mine.astype(BF16)
                copy.start()

        if later:
            for e in range(zparts):
                zcopies.append(rcopy(zbuf.at[q, e], zrec.at[side, q, e], z_sem.at[side, e], q, target))

    for m in range(nrow):
        if m < 2:
            pass_on(m)
        if 1 <= m < nrow - 1:
            pass_on(m + 1)
        compute(m)
        if m < nrow - 1:
            chain(m, False)
        if m == 0:
            share = wbuf[g].astype(F32)
            for j in range(group - 1):
                wcopies[j].wait()
                share = share + wrec[j].astype(F32)
            shard_buf[...] = share.astype(BF16)
            scopies = []
            for j in range(1, nrow):
                scopies.append(rcopy(shard_buf, srec.at[j - 1], s_sem, j - 1, to_row(j)))
                scopies[-1].start()
        else:
            chain(m - 1, True)
        if m == 2:
            for j in range(nrow - 1):
                scopies[j].wait()
                share = share + srec[j].astype(F32)
            wall[g] = share
            gcopies = []
            for j in range(1, group):
                gcopies.append(rcopy(wall.at[g], wall.at[g], g_sem, j - 1, to_group(j)))
                gcopies[-1].start()

    for side in range(2):

        @pl.when(r > 0 if side == 1 else r < nrow - 1)
        def _(side=side):
            for e in range(zparts):
                came = rcopy(
                    zbuf.at[r, e], zrec.at[side, r, e], z_sem.at[side, e], r, {"row": (r + 1) % nrow}
                )
                came.wait_recv()
                cols = slice(e * zcols, (e + 1) * zcols)
                total[nrow - 1, :, cols] = total[nrow - 1, :, cols] + zrec[side, r, e].astype(F32)

    igrad_out[...] = total[nrow - 1].astype(BF16)
    for copy in zcopies:
        copy.wait_send()
    for copy in gcopies:
        copy.wait()
    wgrad_out[...] = wall[...].reshape(width, width)


def keep_kernel(a_in, b_in, c_in, a_out, b_out, c_out):
    a_out[...] = a_in[...]
    b_out[...] = b_in[...]
    c_out[...] = c_in[...]


def local_kernel(sizes, features, weight, cotangent, block_values, block_coords, block_counts):
    nrow, ncol, nrep = sizes
    group = ncol * nrep
    chips = group // 2
    blocks = block_values[0, 0]
    slots = blocks.shape[0]
    nodes, width = cotangent.shape
    col_nodes, fw = features.shape
    row_blocks = nodes * group // 128
    places = row_blocks * (col_nodes // 128)
    chunks = math.gcd(slots, 8)
    srows = width // group
    square = (nodes, width)
    zparts = 2
    half = (nodes // 2, 2 * fw)
    vmem = functools.partial(pl.BlockSpec, memory_space=pltpu.VMEM)
    dma = pltpu.SemaphoreType.DMA
    outs = pl.pallas_call(
        functools.partial(layer_kernel, sizes),
        out_shape=(
            jax.ShapeDtypeStruct(square, BF16),
            jax.ShapeDtypeStruct((fw, col_nodes), BF16),
            jax.ShapeDtypeStruct((width, width), F32),
        ),
        in_specs=[
            pl.BlockSpec(memory_space=pltpu.SMEM),
            vmem(),
            vmem(),
            vmem(),
            vmem(),
            pl.BlockSpec(memory_space=pl.ANY),
        ],
        out_specs=(vmem(), vmem(), vmem()),
        scratch_shapes=[
            pltpu.VMEM((nrow, fw, col_nodes), BF16),
            pltpu.VMEM((slots, 128, 128), BF16),
            pltpu.VMEM((slots + 1, 128, 128), F32),
            pltpu.VMEM((row_blocks * 128, col_nodes), BF16),
            pltpu.VMEM((nrow,) + half, BF16),
            pltpu.VMEM((nrow, chips) + half, BF16),
            pltpu.VMEM((nrow, chips) + half, BF16),
            pltpu.VMEM((nrow, chips - 1) + half, BF16),
            pltpu.VMEM((nrow, chips - 1) + half, BF16),
            pltpu.VMEM((nrow, fw, nodes), BF16),
            pltpu.VMEM((nrow, chips - 1, fw, nodes), BF16),
            pltpu.VMEM((nrow, chips, fw, nodes), BF16),
            pltpu.VMEM((nrow, fw, col_nodes), F32),
            pltpu.VMEM((nrow, zparts, fw, col_nodes // zparts), BF16),
            pltpu.VMEM((2, nrow, zparts, fw, col_nodes // zparts), BF16),
            pltpu.VMEM((group, srows, width), BF16),
            pltpu.VMEM((group - 1, srows, width), BF16),
            pltpu.VMEM((srows, width), BF16),
            pltpu.VMEM((nrow - 1, srows, width), BF16),
            pltpu.VMEM((group, srows, width), F32),
            pltpu.VMEM((1, slots + places), jnp.int32),
            pltpu.SMEM((1, slots + places), jnp.int32),
            dma((chunks,)),
            dma,
            dma((2, 2, nrow)),
            dma((2, nrow)),
            dma((nrow, 2, chips - 1)),
            dma((nrow, 2, chips - 1)),
            dma((nrow, 2, chips)),
            dma((2, zparts, 2, nrow)),
            dma((2, group - 1)),
            dma((2, nrow - 1)),
            dma((2, group - 1)),
        ],
        compiler_params=pltpu.CompilerParams(
            collective_id=0, has_side_effects=True, vmem_limit_bytes=VMEM_BUDGET
        ),
    )(block_counts, block_coords[0, 0].T, features.T, weight, cotangent, blocks)
    activations, input_grad_t, weight_grad = pl.pallas_call(
        keep_kernel,
        out_shape=tuple(jax.ShapeDtypeStruct(x.shape, x.dtype) for x in outs),
        in_specs=[vmem()] * 3,
        out_specs=(vmem(),) * 3,
    )(*outs)
    return activations, input_grad_t.T, weight_grad


def fits(mesh, features, weight, cotangent, block_values):
    nrow, ncol, nrep = (mesh.shape[name] for name in ("row", "col", "rep"))
    group = ncol * nrep
    width = features.shape[1]
    fw = width // nrow
    rows, cols = cotangent.shape[0] // nrow, features.shape[0] // group
    tile = rows * cols * 2 + block_values.shape[2] * 128 * 128 * 6
    moved = 8 * rows * width + 12 * cols * width
    whole = nrep % 2 == 0 and block_values.shape[2] == 128 and rows * cols % 128**3 == 0
    whole = whole and 2 * fw == 128 and nrow > 2 and width % (16 * group) == 0
    return whole and nrow > 1 and group > 2 and tile + moved < VMEM_BUDGET * 3 // 4


def solution(mesh):
    in_specs = (
        P(("col", "rep"), "row"),
        P(),
        P(("row", "col", "rep"), None),
        P("row", ("col", "rep"), None, None, None),
        P("row", ("col", "rep"), None, None),
        P("row", ("col", "rep")),
    )
    out_specs = (P(("row", "col", "rep"), None), P(("col", "rep"), "row"), P())
    sizes = tuple(mesh.shape[name] for name in ("row", "col", "rep"))

    def run(features, weight, cotangent, block_values, block_coords, block_counts):
        if fits(mesh, features, weight, cotangent, block_values):
            body = functools.partial(local_kernel, sizes)
        else:
            body = local_xla
        return jax.shard_map(
            body, mesh=mesh, in_specs=in_specs, out_specs=out_specs, check_vma=False
        )(features, weight, cotangent, block_values, block_coords, block_counts)

    return run
```

```python
import functools
import math

import jax
import jax.numpy as jnp
from jax import lax
from jax.experimental import pallas as pl
from jax.experimental.pallas import tpu as pltpu
from jax.sharding import PartitionSpec as P


def local_xla(features, weight, cotangent, block_values, block_coords, block_counts):
    blocks = block_values[0, 0]
    coords = block_coords[0, 0]
    live_count = block_counts[0, 0]
    slots = blocks.shape[0]
    gathered = lax.all_gather(features, "row", axis=1, tiled=True)
    feat_width = gathered.shape[1]
    col_blocks = gathered.shape[0] // 128
    row_blocks = cotangent.shape[0] * lax.axis_size(("col", "rep")) // 128
    feat_blocks = gathered.reshape(col_blocks, 128, feat_width)
    is_live = (jnp.arange(slots, dtype=jnp.int32) < live_count).astype(jnp.float32)
    per_turn = math.gcd(slots, 64)
    rounds = slots // per_turn
    pieces = (
        blocks.reshape(rounds, per_turn, 128, 128),
        coords[:, 0].reshape(rounds, per_turn),
        coords[:, 1].reshape(rounds, per_turn),
        is_live.reshape(rounds, per_turn),
    )

    def forward_step(total, piece):
        blocks_g, rows_g, cols_g, live_g = piece
        chosen = feat_blocks[cols_g]
        product = jnp.einsum("bij,bjf->bif", blocks_g, chosen, preferred_element_type=jnp.float32)
        return (total.at[rows_g].add(product * live_g[:, None, None]), None)

    partial_value, _ = lax.scan(
        forward_step, jnp.zeros((row_blocks, 128, feat_width), jnp.float32), pieces
    )
    partial_value = partial_value.reshape(row_blocks * 128, feat_width)
    summed = lax.psum_scatter(partial_value, ("col", "rep"), scatter_dimension=0, tiled=True)
    aggregate = summed.astype(jnp.bfloat16)
    pre_act = jnp.dot(aggregate, weight, preferred_element_type=jnp.float32)
    sigma = jax.nn.sigmoid(pre_act)
    activations = (pre_act * sigma).astype(jnp.bfloat16)
    grad_pre = (cotangent.astype(jnp.float32) * sigma * (1.0 + pre_act * (1.0 - sigma))).astype(
        jnp.bfloat16
    )
    weight_terms = jnp.dot(aggregate.T, grad_pre, preferred_element_type=jnp.float32)
    share = lax.psum_scatter(
        weight_terms.astype(jnp.bfloat16), ("col", "rep"), scatter_dimension=0, tiled=True
    ).astype(jnp.float32)
    share = lax.psum(share, "row")
    weight_grad = lax.all_gather(share, ("col", "rep"), axis=0, tiled=True)
    back_rows = jnp.dot(grad_pre, weight.T, preferred_element_type=jnp.float32).astype(jnp.bfloat16)
    back_all = lax.all_gather(back_rows, ("col", "rep"), axis=0, tiled=True)
    back_blocks = back_all.reshape(row_blocks, 128, back_all.shape[1])

    def backward_step(total, piece):
        blocks_g, rows_g, cols_g, live_g = piece
        chosen = back_blocks[rows_g]
        product = jnp.einsum("bji,bjf->bif", blocks_g, chosen, preferred_element_type=jnp.float32)
        return (total.at[cols_g].add(product * live_g[:, None, None]), None)

    grad_terms, _ = lax.scan(
        backward_step, jnp.zeros((col_blocks, 128, back_all.shape[1]), jnp.float32), pieces
    )
    grad_terms = grad_terms.reshape(col_blocks * 128, back_all.shape[1])
    input_grad = lax.psum_scatter(
        grad_terms.astype(jnp.bfloat16), "row", scatter_dimension=1, tiled=True
    )
    return (activations, input_grad, weight_grad)


BF16 = jnp.bfloat16
F32 = jnp.float32
VMEM_BUDGET = 60 * 2**20
MESH = pl.DeviceIdType.MESH


def dot(a, b, ca=1, cb=0):
    return lax.dot_general(a, b, (((ca,), (cb,)), ((), ())), preferred_element_type=F32)


def layer_kernel(
    sizes,
    count_in,
    coords_in,
    feat_in,
    weight_in,
    cot_in,
    blocks_hbm,
    act_out,
    igrad_out,
    wgrad_out,
    fbuf,
    bbuf,
    sums,
    dense,
    feat,
    pbuf,
    prec,
    qbuf,
    qrec,
    own_back,
    brec,
    bpar,
    total,
    zbuf,
    zrec,
    wbuf,
    wrec,
    shard_buf,
    srec,
    wall,
    tvec,
    table,
    load_sem,
    t_sem,
    f_sem,
    p_sem,
    q_sem,
    b_sem,
    c_sem,
    z_sem,
    w_sem,
    s_sem,
    g_sem,
):
    nrow, ncol, nrep = sizes
    nh = nrep // 2
    group = ncol * nrep
    slots = bbuf.shape[0]
    nodes, width = act_out.shape
    fw, col_nodes = feat_in.shape
    row_blocks, col_blocks = dense.shape[0] // 128, dense.shape[1] // 128
    r, c, p = lax.axis_index("row"), lax.axis_index("col"), lax.axis_index("rep")
    h, k = p // 2, p % 2
    g = c * nrep + p
    partner = h * 2 + (1 - k)
    offsets = [(dc, dh) for dc in reversed(range(ncol)) for dh in reversed(range(nh))]
    chips = len(offsets)

    def to_row(j):
        return {"row": (r + j) % nrow}

    def to_group(j):
        q = (g + j) % group
        return {"col": q // nrep, "rep": q % nrep}

    def to_chip(i):
        dc, dh = offsets[i]
        return {"col": (c + dc) % ncol, "rep": ((h + dh) % nh) * 2 + k}

    def part_to(i, core):
        dc, dh = offsets[i]
        return ((c + dc) % ncol) * nrep + ((h + dh) % nh) * 2 + core

    def part_from(i, core):
        dc, dh = offsets[i]
        return ((c + ncol - dc) % ncol) * nrep + ((h + nh - dh) % nh) * 2 + core

    def nearest(n):
        code = 0
        for q in range(nrow):
            order = sorted(range(nrow), key=lambda t: (abs(t - q), t))
            code += order[n] * nrow**q
        power = 1
        for q in range(1, nrow):
            power = power * jnp.where(r >= q, nrow, 1)
        return (code // power) % nrow

    def rcopy(src, dst, sems, i, device):
        return pltpu.make_async_remote_copy(
            src_ref=src,
            dst_ref=dst,
            send_sem=sems.at[0, i],
            recv_sem=sems.at[1, i],
            device_id=device,
            device_id_type=MESH,
        )

    chunks = load_sem.shape[0]
    per = slots // chunks
    loads = []
    for i in range(chunks):
        span = pl.ds(i * per, per)
        loads.append(pltpu.make_async_copy(blocks_hbm.at[span], bbuf.at[span], load_sem.at[i]))
        loads[-1].start()

    barrier = pltpu.get_barrier_semaphore()
    for j in range(1, nrow):
        pl.semaphore_signal(barrier, inc=1, device_id=to_row(j), device_id_type=MESH)
    for j in range(1, group):
        pl.semaphore_signal(barrier, inc=1, device_id=to_group(j), device_id_type=MESH)

    pl.semaphore_wait(barrier, nrow - 1 + group - 1)
    fcopies = []
    for side in range(2):
        there = r > 0 if side == 0 else r < nrow - 1
        copy = rcopy(feat_in, fbuf.at[r], f_sem.at[side], r, {"row": (r + nrow - 1 + 2 * side) % nrow})
        fcopies.append((there, copy))

        @pl.when(there)
        def _(copy=copy):
            copy.start()

    def relay(n):
        slot = nearest(n)
        side = (slot < r).astype(jnp.int32)
        there = jnp.where(slot < r, r < nrow - 1, r > 0)
        copy = rcopy(
            fbuf.at[slot], fbuf.at[slot], f_sem.at[side], slot, {"row": (r + nrow - 1 + 2 * side) % nrow}
        )
        copy.wait_recv()
        fcopies.append((there, copy))

        @pl.when(there)
        def _():
            copy.start()

    fbuf[r] = feat_in[...]

    places = row_blocks * col_blocks
    live = count_in[0, 0]
    row_form = coords_in[0:1, :] * col_blocks + coords_in[1:2, :]
    column_form = jnp.broadcast_to(row_form, (slots, slots)).T
    mine_at = lax.broadcasted_iota(jnp.int32, (slots, slots), 0)
    other_at = lax.broadcasted_iota(jnp.int32, (slots, slots), 1)
    hit = (column_form == row_form) & (mine_at < jnp.minimum(other_at, live))
    tvec[0:1, 0:slots] = jnp.max(jnp.where(hit, mine_at + 1, 0), axis=0, keepdims=True)
    for start in range(0, places, slots):
        hit = (column_form == other_at + start) & (mine_at < live)
        tvec[0:1, slots + start : 2 * slots + start] = jnp.max(
            jnp.where(hit, mine_at + 1, 0), axis=0, keepdims=True
        )
    tcopy = pltpu.make_async_copy(tvec, table, t_sem)
    tcopy.start()
    tcopy.wait()

    sums[0] = jnp.zeros((128, 128), F32)
    for i in range(chunks):
        loads[i].wait()

        def add_slot(s, carry):
            sums[s + 1] = sums[table[0, s]] + bbuf[s].astype(F32)
            return carry

        lax.fori_loop(i * per, (i + 1) * per, add_slot, 0)
        if i == chunks // 2 - 1:
            relay(1)
    relay(2)

    def fill(rb, carry):
        for cb in range(col_blocks):
            block = sums[table[0, slots + rb * col_blocks + cb]]
            dense[pl.ds(rb * 128, 128), cb * 128 : (cb + 1) * 128] = block.astype(BF16)
        return carry

    lax.fori_loop(0, row_blocks, fill, 0)

    half = nodes // 2

    def partial(part, slot):
        x = dot(dense[pl.ds(part * nodes, nodes), :], fbuf[slot], 1, 1)
        return jnp.concatenate([x[:half], x[half:]], axis=1)

    qcopies = []

    def merge(n, pcopy, mine):
        pcopy.wait()
        for i in range(chips - 1):
            qbuf[n, i] = (mine[i] + prec[n, i].astype(F32)).astype(BF16)
            copy = rcopy(qbuf.at[n, i], qrec.at[n, i], q_sem.at[n], i, to_chip(i))
            copy.start()
            qcopies.append(copy)
        return mine[chips - 1] + prec[n, chips - 1].astype(F32)

    held, waiting = [], None
    for n in range(nrow):
        slot = nearest(n)
        for i in range(chips):
            pbuf[n, i] = partial(part_to(i, 1 - k), slot).astype(BF16)
        pcopy = rcopy(pbuf.at[n], prec.at[n], p_sem, n, {"rep": partner})
        pcopy.start()
        if waiting is not None:
            held.append(merge(*waiting))
        waiting = (n, pcopy, [partial(part_to(i, k), slot) for i in range(chips)])
        if 3 <= n + 2 < nrow:
            relay(n + 2)
    held.append(merge(*waiting))
    for there, copy in fcopies:

        @pl.when(there)
        def _(copy=copy):
            copy.wait_send()

    for n in range(nrow):
        got = held[n]
        for i in range(chips - 1):
            qcopies[n * (chips - 1) + i].wait()
            got = got + qrec[n, i].astype(F32)
        feat[nearest(n)] = got.astype(BF16)

    spread = jnp.concatenate([feat[m] for m in range(nrow)], axis=1)
    pieces = [spread[:, m * fw : (m + 1) * fw] for m in range(2 * nrow)]
    aggregate = jnp.concatenate(
        [jnp.concatenate(pieces[0::2], axis=1), jnp.concatenate(pieces[1::2], axis=1)], axis=0
    )
    pre_act = dot(aggregate, weight_in[...])
    sigma = jax.nn.sigmoid(pre_act)
    grad_pre = (cot_in[...].astype(F32) * sigma * (1.0 + pre_act * (1.0 - sigma))).astype(BF16)
    own_back[...] = dot(weight_in[...], grad_pre, 1, 1).astype(BF16)
    bcopies, ccopies = [], []
    for i in range(chips - 1):
        bcopies.append(rcopy(own_back, brec.at[i], b_sem, i, to_chip(i)))
        bcopies[i].start()
    first = rcopy(own_back, bpar.at[chips - 1], c_sem, chips - 1, {"rep": partner})
    first.start()

    terms = dot(aggregate, grad_pre, 0, 0)
    srows = width // group
    wbuf[...] = terms.astype(BF16).reshape(group, srows, width)
    wcopies = []
    for j in range(1, group):
        wcopies.append(rcopy(wbuf.at[(g + j) % group], wrec.at[j - 1], w_sem, j - 1, to_group(j)))
        wcopies[-1].start()
    act_out[...] = (pre_act * sigma).astype(BF16)

    def back_term(piece_t, part):
        return dot(piece_t, dense[pl.ds(part * nodes, nodes), :])

    total[...] = back_term(own_back[...], g)
    first.wait()
    total[...] += back_term(bpar[chips - 1], c * nrep + partner)

    for i in reversed(range(chips - 1)):
        bcopies[i].wait()
        ccopies.append(rcopy(brec.at[i], bpar.at[i], c_sem, i, {"rep": partner}))
        ccopies[-1].start()
        total[...] += back_term(brec[i], part_from(i, k))

    share = wbuf[g].astype(F32)
    for j in range(group - 1):
        wcopies[j].wait()
        share = share + wrec[j].astype(F32)
    shard_buf[...] = share.astype(BF16)
    scopies = []
    for j in range(1, nrow):
        scopies.append(rcopy(shard_buf, srec.at[j - 1], s_sem, j - 1, to_row(j)))
        scopies[-1].start()

    for n, i in enumerate(reversed(range(chips - 1))):
        ccopies[n].wait()
        total[...] += back_term(bpar[i], part_from(i, 1 - k))

    zcopies = []
    for j in range(1, nrow):
        q = (r + j) % nrow
        zbuf[j - 1] = total[pl.ds(q * fw, fw), :].astype(BF16)
        zcopies.append(rcopy(zbuf.at[j - 1], zrec.at[j - 1], z_sem, j - 1, to_row(j)))
        zcopies[-1].start()

    for j in range(nrow - 1):
        scopies[j].wait()
        share = share + srec[j].astype(F32)
    wall[g] = share
    gcopies = []
    for j in range(1, group):
        gcopies.append(rcopy(wall.at[g], wall.at[g], g_sem, j - 1, to_group(j)))
        gcopies[-1].start()

    mine = total[pl.ds(r * fw, fw), :]
    for j in range(nrow - 1):
        zcopies[j].wait()
        mine = mine + zrec[j].astype(F32)
    igrad_out[...] = mine.astype(BF16)
    for copy in gcopies:
        copy.wait()
    wgrad_out[...] = wall[...].reshape(width, width)


def keep_kernel(a_in, b_in, c_in, a_out, b_out, c_out):
    a_out[...] = a_in[...]
    b_out[...] = b_in[...]
    c_out[...] = c_in[...]


def local_kernel(sizes, features, weight, cotangent, block_values, block_coords, block_counts):
    nrow, ncol, nrep = sizes
    group = ncol * nrep
    chips = group // 2
    blocks = block_values[0, 0]
    slots = blocks.shape[0]
    nodes, width = cotangent.shape
    col_nodes, fw = features.shape
    row_blocks = nodes * group // 128
    places = row_blocks * (col_nodes // 128)
    chunks = math.gcd(slots, 8)
    srows = width // group
    square = (nodes, width)
    half = (nodes // 2, 2 * fw)
    vmem = functools.partial(pl.BlockSpec, memory_space=pltpu.VMEM)
    dma = pltpu.SemaphoreType.DMA
    outs = pl.pallas_call(
        functools.partial(layer_kernel, sizes),
        out_shape=(
            jax.ShapeDtypeStruct(square, BF16),
            jax.ShapeDtypeStruct((fw, col_nodes), BF16),
            jax.ShapeDtypeStruct((width, width), F32),
        ),
        in_specs=[
            pl.BlockSpec(memory_space=pltpu.SMEM),
            vmem(),
            vmem(),
            vmem(),
            vmem(),
            pl.BlockSpec(memory_space=pl.ANY),
        ],
        out_specs=(vmem(), vmem(), vmem()),
        scratch_shapes=[
            pltpu.VMEM((nrow, fw, col_nodes), BF16),
            pltpu.VMEM((slots, 128, 128), BF16),
            pltpu.VMEM((slots + 1, 128, 128), F32),
            pltpu.VMEM((row_blocks * 128, col_nodes), BF16),
            pltpu.VMEM((nrow,) + half, BF16),
            pltpu.VMEM((nrow, chips) + half, BF16),
            pltpu.VMEM((nrow, chips) + half, BF16),
            pltpu.VMEM((nrow, chips - 1) + half, BF16),
            pltpu.VMEM((nrow, chips - 1) + half, BF16),
            pltpu.VMEM((width, nodes), BF16),
            pltpu.VMEM((chips - 1, width, nodes), BF16),
            pltpu.VMEM((chips, width, nodes), BF16),
            pltpu.VMEM((width, col_nodes), F32),
            pltpu.VMEM((nrow - 1, fw, col_nodes), BF16),
            pltpu.VMEM((nrow - 1, fw, col_nodes), BF16),
            pltpu.VMEM((group, srows, width), BF16),
            pltpu.VMEM((group - 1, srows, width), BF16),
            pltpu.VMEM((srows, width), BF16),
            pltpu.VMEM((nrow - 1, srows, width), BF16),
            pltpu.VMEM((group, srows, width), F32),
            pltpu.VMEM((1, slots + places), jnp.int32),
            pltpu.SMEM((1, slots + places), jnp.int32),
            dma((chunks,)),
            dma,
            dma((2, 2, nrow)),
            dma((2, nrow)),
            dma((nrow, 2, chips - 1)),
            dma((2, chips - 1)),
            dma((2, chips)),
            dma((2, nrow - 1)),
            dma((2, group - 1)),
            dma((2, nrow - 1)),
            dma((2, group - 1)),
        ],
        compiler_params=pltpu.CompilerParams(
            collective_id=0, has_side_effects=True, vmem_limit_bytes=VMEM_BUDGET
        ),
    )(block_counts, block_coords[0, 0].T, features.T, weight, cotangent, blocks)
    activations, input_grad_t, weight_grad = pl.pallas_call(
        keep_kernel,
        out_shape=tuple(jax.ShapeDtypeStruct(x.shape, x.dtype) for x in outs),
        in_specs=[vmem()] * 3,
        out_specs=(vmem(),) * 3,
    )(*outs)
    return activations, input_grad_t.T, weight_grad


def fits(mesh, features, weight, cotangent, block_values):
    nrow, ncol, nrep = (mesh.shape[name] for name in ("row", "col", "rep"))
    group = ncol * nrep
    width = features.shape[1]
    fw = width // nrow
    rows, cols = cotangent.shape[0] // nrow, features.shape[0] // group
    tile = rows * cols * 2 + block_values.shape[2] * 128 * 128 * 6
    moved = 8 * rows * width + 12 * cols * width
    whole = nrep % 2 == 0 and block_values.shape[2] == 128 and rows * cols % 128**3 == 0
    whole = whole and 2 * fw == 128 and nrow > 2 and width % (16 * group) == 0
    return whole and nrow > 1 and group > 2 and tile + moved < VMEM_BUDGET * 3 // 4


def solution(mesh):
    in_specs = (
        P(("col", "rep"), "row"),
        P(),
        P(("row", "col", "rep"), None),
        P("row", ("col", "rep"), None, None, None),
        P("row", ("col", "rep"), None, None),
        P("row", ("col", "rep")),
    )
    out_specs = (P(("row", "col", "rep"), None), P(("col", "rep"), "row"), P())
    sizes = tuple(mesh.shape[name] for name in ("row", "col", "rep"))

    def run(features, weight, cotangent, block_values, block_coords, block_counts):
        if fits(mesh, features, weight, cotangent, block_values):
            body = functools.partial(local_kernel, sizes)
        else:
            body = local_xla
        return jax.shard_map(
            body, mesh=mesh, in_specs=in_specs, out_specs=out_specs, check_vma=False
        )(features, weight, cotangent, block_values, block_coords, block_counts)

    return run
```
